128 devices in a mesh: sec: 4 (over y_hi, core), tile: 32 (over x, y_lo, z).
Axes of the slice: x: 4, y: 4 (y_hi: 2, y_lo: 2; y = y_hi * 2 + y_lo), z: 4, core: 2. Of those that a mesh axis runs over, the one named last changes fastest.
Arguments:
- displacement: float32 [2, 64, 512, 2048], P(None, 'sec', 'tile'), may hold values from -6 to 6
- stiff_right: float32 [64, 512, 2048], P('sec', 'tile'), may hold values from 0.3 to 3
- stiff_down: float32 [64, 512, 2048], P('sec', 'tile'), may hold values from 0.3 to 3
- bilinear: float32 [128], replicated, may hold values from 0.15 to 0.6
- match_source: int32 [128, 3, 3, 32], P(('sec', 'tile')), may hold values from 0 to 4095, as said below
- match_target: int32 [128, 3, 3, 32], P(('sec', 'tile')), may hold values from 0 to 4095
- match_count: int32 [128, 3, 3], P(('sec', 'tile')), may hold values from 0 to 32, as said below
- match_weight: float32 [128, 3, 3, 32], P(('sec', 'tile')), may hold values from 0.3 to 3
Outputs:
- relaxed: float32 [2, 64, 512, 2048], P(None, 'sec', 'tile')
The draws below stay inside these ranges and needn't reach their ends.
Inputs may be any that keep to these rules, and one draw needn't show every extreme that they name: `match_count`: counts toward owners that do not exist are 0. Every source device has 32 live slots toward some existing neighbouring owner, and one device receives 32 live slots from each of its neighbours and itself; slots at or past the count are ignored. `match_source`: the source block and the target block of every slot lie in adjacent sections, at most two node rows and one block column apart in the whole stack.
All inputs are finite; a program needn't handle non-finite values.
Results may differ from the reference program's by a relative error of at most 0.00002.
Values sent between devices are 32-bit elements; how exact they have to be, the bound alone decides.
No kernel may reach another device: no remote copies, remote signals or barrier semaphores. Data moves between devices by JAX's collectives and lax.ppermute only.
A program may use at most 128 MiB of HBM per device.

```python
import math
import jax
import jax.numpy as jnp

S_DEV = 16
R_DEV = 16
W = 2048
CAP = 32
ITERS = 4
SECTIONS = 64
ROWS = 512
PEERS = 128
N_SEC = 4
N_TILE = 32


def draw_pairs(key):
    base = jax.random.fold_in(key, 21)
    keys = [jax.random.fold_in(base, number) for number in range(8)]
    shape = (PEERS, 3, 3, CAP)
    blocks_row = W // 128
    sec_offset = (jnp.arange(3) - 1)[None, :, None, None]
    tile_offset = (jnp.arange(3) - 1)[None, None, :, None]
    sec_in = jax.random.randint(keys[0], shape, 0, S_DEV)
    direction = jnp.where(jax.random.randint(keys[1], shape, 0, 2) == 0, -1, 1)
    direction = jnp.where(sec_in == 0, 1, jnp.where(sec_in == S_DEV - 1, -1, direction))
    src_sec = jnp.where(sec_offset == 0, sec_in, jnp.where(sec_offset > 0, S_DEV - 1, 0))
    tgt_sec = jnp.where(sec_offset == 0, sec_in + direction, jnp.where(sec_offset > 0, 0, S_DEV - 1))
    row_in = jax.random.randint(keys[2], shape, 0, R_DEV)
    row_move = jax.random.randint(keys[3], shape, -2, 3)
    near_edge = jax.random.randint(keys[4], shape, 0, 2)
    far_edge = jax.random.randint(keys[5], shape, 0, 2) * (1 - near_edge)
    src_row = jnp.where(tile_offset == 0, row_in, jnp.where(tile_offset > 0, R_DEV - 1 - near_edge, near_edge))
    tgt_row = jnp.where(tile_offset == 0, jnp.clip(row_in + row_move, 0, R_DEV - 1), jnp.where(tile_offset > 0, far_edge, R_DEV - 1 - far_edge))
    col_in = jax.random.randint(keys[6], shape, 0, blocks_row)
    col_move = jax.random.randint(keys[7], shape, -1, 2)
    tgt_col = jnp.clip(col_in + col_move, 0, blocks_row - 1)
    source = (src_sec * R_DEV + src_row) * blocks_row + col_in
    target = (tgt_sec * R_DEV + tgt_row) * blocks_row + tgt_col
    return (source.astype(jnp.int32), target.astype(jnp.int32))


def draw_match_source(key, part):
    return draw_pairs(key)[0]


def draw_match_target(key, part):
    return draw_pairs(key)[1]


def draw_match_count(key, part):
    key_level = jax.random.fold_in(key, 11)
    key_count = jax.random.fold_in(key, 12)
    key_hot = jax.random.fold_in(key, 13)
    key_partner = jax.random.fold_in(key, 14)
    tile_count = ROWS // R_DEV
    sec_count = PEERS // tile_count
    peer = jnp.arange(PEERS)
    offset = jnp.arange(3) - 1
    owner_sec = (peer // tile_count)[:, None, None] + offset[None, :, None]
    owner_tile = (peer % tile_count)[:, None, None] + offset[None, None, :]
    valid = (owner_sec >= 0) & (owner_sec < sec_count) & (owner_tile >= 0) & (owner_tile < tile_count)
    owner = owner_sec * tile_count + owner_tile
    level = jax.random.randint(key_level, (PEERS, 1, 1), 2, 5)
    top = CAP * level // 4
    counts = jax.random.randint(key_count, (PEERS, 3, 3), 0, top + 1)
    hot = jax.random.randint(key_hot, (), 0, PEERS)
    partner = jax.random.randint(key_partner, (PEERS,), 0, 9)
    place = jnp.arange(9).reshape(1, 3, 3)
    partner_ok = jnp.take_along_axis(valid.reshape(PEERS, 9), partner[:, None], axis=1)[:, 0]
    partner = jnp.where(partner_ok, partner, 4)
    counts = jnp.where((owner == hot) & valid, CAP, counts)
    counts = jnp.where(place == partner[:, None, None], CAP, counts)
    counts = jnp.where(valid, counts, 0)
    return counts.astype(jnp.int32)


def steps_of(stream_key, dims, cuts, smallest, largest):
    def one(dim, blocks):
        heights = jax.random.uniform(jax.random.fold_in(jax.random.fold_in(stream_key, 6), dim), (blocks,), jnp.float32, smallest / len(cuts), largest / len(cuts))
        return jnp.repeat(jnp.exp(heights), dims[dim] // blocks).reshape((-1,) + (1,) * (len(dims) - dim - 1))

    gain = one(*cuts[0])
    for cut in cuts[1:]:
        gain = gain * one(*cut)
    return gain


def noise(stream_key, extent, deviation, most, shards=(), held_as=jnp.bfloat16):
    drawn = jax.random.normal(stream_key, extent, jnp.float32) * deviation
    if len(shards) > 0:
        drawn = steps_of(stream_key, extent, shards, -0.22, 0.18) * drawn
    return jnp.clip(drawn, min=-most, max=most).astype(held_as)


def setup_inputs(seed: int = 0) -> dict:
    arg_keys = jax.random.split(jax.random.key(seed), 9)
    displacement = noise(arg_keys[0], (2, SECTIONS, ROWS, W), 1.0, 6.0, ((1, 4), (2, 32)), jnp.float32)
    stiff_right = jnp.clip(jnp.exp(math.log(3.0) - 2.3025851 * jax.random.uniform(arg_keys[1], (SECTIONS, ROWS, W), jnp.float32) ** steps_of(arg_keys[1], (SECTIONS, ROWS, W), ((0, 4), (1, 32)), -0.2, 0.2)), 0.3, 3.0)
    stiff_down = jnp.clip(jnp.exp(math.log(3.0) - 2.3025851 * jax.random.uniform(arg_keys[2], (SECTIONS, ROWS, W), jnp.float32) ** steps_of(arg_keys[2], (SECTIONS, ROWS, W), ((0, 4), (1, 32)), -0.2, 0.2)), 0.3, 3.0)
    bilinear = jnp.clip(jnp.exp(jax.random.uniform(arg_keys[3], (128,), jnp.float32, math.log(0.15), math.log(0.6))), 0.15, 0.6)
    match_source = draw_match_source(jax.random.fold_in(arg_keys[8], 71), 0)
    match_target = draw_match_target(jax.random.fold_in(arg_keys[8], 71), 0)
    match_count = draw_match_count(jax.random.fold_in(arg_keys[8], 71), 0)
    match_weight = jnp.clip(jnp.exp(math.log(3.0) - 2.3025851 * jax.random.uniform(arg_keys[7], (PEERS, 3, 3, CAP), jnp.float32) ** steps_of(arg_keys[7], (PEERS, 3, 3, CAP), ((0, 128),), -0.2, 0.2)), 0.3, 3.0)
    return dict(displacement=displacement, stiff_right=stiff_right, stiff_down=stiff_down, bilinear=bilinear, match_source=match_source, match_target=match_target, match_count=match_count, match_weight=match_weight)


def global_block(local, device):
    blocks_row = W // 128
    sec_pos = device // N_TILE
    tile_pos = device % N_TILE
    section = sec_pos * S_DEV + local // (R_DEV * blocks_row)
    row = tile_pos * R_DEV + (local // blocks_row) % R_DEV
    column = local % blocks_row
    return ((section * ROWS + row) * blocks_row + column).astype(jnp.int32)


def resample(blocks, bilinear):
    following = jnp.concatenate([blocks[..., 1:], blocks[..., -1:]], axis=-1)
    return blocks + bilinear * (following - blocks)


def spring_force(field, k_right, k_left, k_down, k_up):
    zero_col = jnp.zeros(field.shape[:-1] + (1,), jnp.float32)
    zero_row = jnp.zeros(field.shape[:-2] + (1, field.shape[-1]), jnp.float32)
    right = jnp.concatenate([field[..., 1:], zero_col], axis=-1)
    left = jnp.concatenate([zero_col, field[..., :-1]], axis=-1)
    below = jnp.concatenate([field[:, :, 1:, :], zero_row], axis=2)
    above = jnp.concatenate([zero_row, field[:, :, :-1, :]], axis=2)
    return k_right * (right - field) + k_left * (left - field) + k_down * (below - field) + k_up * (above - field)


def reference(displacement, stiff_right, stiff_down, bilinear, match_source, match_target, match_count, match_weight):
    blocks_row = W // 128
    total_blocks = SECTIONS * ROWS * blocks_row
    peer = jnp.arange(PEERS, dtype=jnp.int32)
    sec_pos = peer // N_TILE
    tile_pos = peer % N_TILE
    offset = jnp.arange(3, dtype=jnp.int32) - 1
    owner_sec = sec_pos[:, None, None] + offset[None, :, None]
    owner_tile = tile_pos[:, None, None] + offset[None, None, :]
    valid = (owner_sec >= 0) & (owner_sec < N_SEC) & (owner_tile >= 0) & (owner_tile < N_TILE)
    owner = (jnp.clip(owner_sec, 0, N_SEC - 1) * N_TILE + jnp.clip(owner_tile, 0, N_TILE - 1)).astype(jnp.int32)
    gsrc = global_block(match_source, peer[:, None, None, None]).reshape(-1)
    gtgt = global_block(match_target, owner[:, :, :, None]).reshape(-1)
    live = (jnp.arange(CAP, dtype=jnp.int32)[None, None, None, :] < match_count[:, :, :, None]) & valid[:, :, :, None]
    live_weight = jnp.where(live, match_weight, jnp.zeros_like(match_weight)).reshape(-1)
    k_right = stiff_right.at[:, :, -1].set(0.0)
    k_down = stiff_down.at[:, -1, :].set(0.0)
    k_left = jnp.concatenate([jnp.zeros((SECTIONS, ROWS, 1), jnp.float32), k_right[:, :, :-1]], axis=2)
    k_up = jnp.concatenate([jnp.zeros((SECTIONS, 1, W), jnp.float32), k_down[:, :-1, :]], axis=1)
    match_diag = jnp.zeros((total_blocks,), jnp.float32).at[gsrc].add(live_weight)
    match_diag = jnp.broadcast_to(match_diag[:, None], (total_blocks, 128)).reshape(SECTIONS, ROWS, W)
    diag = 1.0 + k_right + k_left + k_down + k_up + match_diag
    relaxed = displacement
    for step in range(ITERS):
        spring = spring_force(relaxed, k_right, k_left, k_down, k_up)
        blocked = relaxed.reshape(2, total_blocks, 128)
        interp = resample(blocked[:, gtgt], bilinear)
        term = live_weight[None, :, None] * (interp - blocked[:, gsrc])
        matchforce = jnp.zeros((2, total_blocks, 128), jnp.float32).at[:, gsrc].add(term)
        matchforce = matchforce.reshape(2, SECTIONS, ROWS, W)
        relaxed = relaxed + 0.8 * (spring + matchforce) / diag
    return relaxed
```

```python
import jax
import jax.numpy as jnp
from jax import lax
from jax.experimental import pallas as pl
from jax.experimental.pallas import tpu as pltpu
from jax.sharding import PartitionSpec as P

ITERS = 4
SEC = 16
ROW = 16
WID = 2048
LANE = 128
COLS = WID // LANE
CAP = 32
SEG = 3 * CAP
ROWS_MSG = 2 * SEC * COLS
T_MSG = ROWS_MSG + 2 * SEG

VM = pl.BlockSpec(memory_space=pltpu.VMEM)
SM = pl.BlockSpec(memory_space=pltpu.SMEM)


def vmem(*shape):
    return pltpu.VMEM(shape, jnp.float32)


def kernel_call(body, outs, n_smem, n_vmem, aliases=None, scratch=(), cost=0):
    return pl.pallas_call(
        body,
        out_shape=tuple(outs),
        in_specs=[SM] * n_smem + [VM] * n_vmem,
        out_specs=tuple(VM for _ in outs),
        scratch_shapes=list(scratch),
        input_output_aliases=aliases or {},
        compiler_params=pltpu.CompilerParams(vmem_limit_bytes=4 * 2**20),
        cost_estimate=pl.CostEstimate(flops=cost, bytes_accessed=cost, transcendentals=0),
        name=body.__name__,
    )


def swaps(count, first):
    pairs = [(i, i + 1) for i in range(first, count - 1, 2)]
    return pairs + [(j, i) for i, j in pairs]


def exchange(to_a, to_b, axis):
    count = lax.axis_size(axis)
    from_b = lax.ppermute(to_b, axis, swaps(count, 1))
    from_a = lax.ppermute(to_a, axis, swaps(count, 0))
    return from_a, from_b


def place(block):
    return (block >> 8) & 15, block & 15, (block >> 4) & 15


def lanes(j):
    return slice(j * LANE, (j + 1) * LANE)


def iota(dim):
    return lax.broadcasted_iota(jnp.int32, (ROW, LANE), dim)


def setup_kernel(src, weight, keep, kr_in, kd_in, kr_ref, kd_ref, dg_ref, rim_ref):
    lane, row = iota(1), iota(0)
    kept = keep[0]

    def section(s, _):
        before = jnp.zeros((ROW, LANE), jnp.float32)
        for j in range(COLS):
            kr = kr_in[s, :, lanes(j)]
            if j == COLS - 1:
                kr = jnp.where(lane == LANE - 1, 0.0, kr)
            kr_ref[s, j] = kr
            turned = pltpu.roll(kr, 1, 1)
            left = jnp.where(lane == 0, before, turned)
            before = turned
            kd = kd_in[s, :, lanes(j)]
            inner = jnp.where(row == ROW - 1, 0.0, kd)
            kd_ref[s, j] = inner
            down = jnp.where(row == ROW - 1, kd * kept, kd)
            rim_ref[pl.ds(j * SEC + s, 1), :] = down[ROW - 1 :, :]
            dg_ref[s, j] = 1.0 + kr + left + down + pltpu.roll(inner, 1, 0)
        return 0

    lax.fori_loop(0, SEC, section, 0)

    def slots(i, _):
        for j in range(8):
            s, c, r = place(src[i * 8 + j])
            dg_ref[s, c, pl.ds(r, 1), :] += weight[i * 8 + j]
        return 0

    lax.fori_loop(0, 9 * CAP // 8, slots, 0)


def load_kernel(field_in, u_ref):
    def section(s, _):
        for m in range(2):
            for j in range(COLS):
                u_ref[m, s, j] = field_in[m, s, :, lanes(j)]
        return 0

    lax.fori_loop(0, SEC, section, 0)


def coefficient_kernel(src, weight, parity, dg_in, got_a, got_b, rim, cc_ref, ca_ref, cb_ref, cw_ref):
    odd = parity[0] == 1

    def column(j, _):
        at = pl.ds(pl.multiple_of(j * SEC, SEC), SEC)
        upper = jnp.where(odd, got_a[at, :], got_b[at, :])
        cc_ref[:, j, 0, :] = dg_in[:, j, 0, :] + upper
        cc_ref[:, j, 1:, :] = dg_in[:, j, 1:, :]
        return 0

    lax.fori_loop(0, COLS, column, 0)

    def section(s, _):
        for j in range(COLS):
            cc_ref[s, j] = 0.8 / cc_ref[s, j]
        return 0

    lax.fori_loop(0, SEC, section, 0)

    def rims(j, _):
        at = pl.ds(pl.multiple_of(j * SEC, SEC), SEC)
        first = cc_ref[:, j, 0, :] * jnp.where(odd, got_a[at, :], got_b[at, :])
        last = cc_ref[:, j, ROW - 1, :] * rim[at, :]
        ca_ref[at, :] = jnp.where(odd, first, last)
        cb_ref[at, :] = jnp.where(odd, last, first)
        return 0

    lax.fori_loop(0, COLS, rims, 0)

    def slots(i, _):
        for j in range(8):
            k = i * 8 + j
            s, c, r = place(src[k])
            cw_ref[pl.ds(k, 1), :] = cc_ref[s, c, pl.ds(r, 1), :] * weight[k]
        return 0

    lax.fori_loop(0, 9 * CAP // 8, slots, 0)


def pack_blocks(wanted, start, count, u_ref, msg_ref, at, stride):
    def slots(i, _):
        for j in range(8):
            k = i * 8 + j
            s, c, r = place(wanted[start + k])
            for m in range(2):
                msg_ref[pl.ds(at + m * stride + k, 1), :] = u_ref[m, s, c, pl.ds(r, 1), :]
        return 0

    lax.fori_loop(0, count // 8, slots, 0)


def each_rows(fn):
    def column(j, _):
        for m in range(2):
            fn(m, j, pl.ds(pl.multiple_of((m * COLS + j) * SEC, SEC), SEC))
        return 0

    lax.fori_loop(0, COLS, column, 0)


def pack_messages(wanted, parity, u_ref, a_ref, b_ref):
    def rows(row_a, row_b):
        def copy(m, j, at):
            a_ref[at, :] = u_ref[m, :, j, row_a, :]
            b_ref[at, :] = u_ref[m, :, j, row_b, :]

        each_rows(copy)

    pl.when(parity[0] == 0)(lambda: rows(ROW - 1, 0))
    pl.when(parity[0] == 1)(lambda: rows(0, ROW - 1))
    pack_blocks(wanted, 0, SEG, u_ref, a_ref, ROWS_MSG, SEG)
    pack_blocks(wanted, SEG, SEG, u_ref, b_ref, ROWS_MSG, SEG)


def pack_kernel(wanted, parity, u_ref, a_ref, b_ref):
    pack_messages(wanted, parity, u_ref, a_ref, b_ref)


def terms(blocks, fraction, scale):
    return scale * (blocks + fraction * (pltpu.roll(blocks, LANE - 1, 1) - blocks))


def scatter(src, start, count, u_ref, term_ref, stride):
    def slots(i, _):
        for j in range(8):
            k = i * 8 + j
            s, c, r = place(src[start + k])
            for m in range(2):
                u_ref[m, s, c, pl.ds(r, 1), :] += term_ref[pl.ds(m * stride + k, 1), :]
        return 0

    lax.fori_loop(0, count // 8, slots, 0)


LOCAL = 4 * CAP


def dense_kernel(src, local_target, wanted_sec, u_in, kr_ref, kd_ref, cc_ref, cw_ref, frac_ref, u_ref, own_a, own_b, term_ref):
    lane = iota(1)

    def section(s, _):
        for m in range(2):
            load = lambda j: u_in[m, s, j]
            here = load(0)
            here_turned = pltpu.roll(here, LANE - 1, 1)
            before = jnp.zeros((ROW, LANE), jnp.float32)
            for j in range(COLS):
                kr = kr_ref[s, j]
                kd = kd_ref[s, j]
                cc = cc_ref[s, j]
                if j + 1 < COLS:
                    after = load(j + 1)
                    after_turned = pltpu.roll(after, LANE - 1, 1)
                    right = jnp.where(lane == LANE - 1, after_turned, here_turned)
                else:
                    after, after_turned, right = None, None, here_turned
                turned = pltpu.roll(kr * here, 1, 1)
                total = here + kr * right + jnp.where(lane == 0, before, turned)
                total = total + kd * pltpu.roll(here, ROW - 1, 0) + pltpu.roll(kd * here, 1, 0)
                u_ref[m, s, j] = 0.2 * here + cc * total
                here, here_turned, before = after, after_turned, turned
        return 0

    lax.fori_loop(0, SEC, section, 0)
    pack_blocks(local_target, 0, CAP, u_in, term_ref, 0, CAP)
    fraction = frac_ref[...]
    scale = cw_ref[pl.ds(LOCAL, CAP), :]
    for m in range(2):
        at = pl.ds(m * CAP, CAP)
        term_ref[at, :] = terms(term_ref[at, :], fraction, scale)
    scatter(src, LOCAL, CAP, u_ref, term_ref, CAP)
    pack_blocks(wanted_sec, 0, CAP, u_in, own_a, 0, CAP)
    pack_blocks(wanted_sec, CAP, CAP, u_in, own_b, 0, CAP)


def relay_kernel(from_a, from_b, own_a, own_b, a_ref, b_ref):
    for m in range(2):
        for out, own, seg in ((a_ref, own_a, 0), (b_ref, own_b, 2)):
            there = ROWS_MSG + m * SEG + seg * CAP
            out[pl.ds(m * SEG, CAP), :] = from_a[pl.ds(there, CAP), :]
            out[pl.ds(m * SEG + CAP, CAP), :] = own[pl.ds(m * CAP, CAP), :]
            out[pl.ds(m * SEG + 2 * CAP, CAP), :] = from_b[pl.ds(there, CAP), :]


def tile_kernel(src, parity, u_in, from_a, from_b, ca_ref, cb_ref, cw_ref, frac_ref, u_ref, term_ref):
    def rows(row_a, row_b):
        def add(m, j, at):
            own = pl.ds(pl.multiple_of(j * SEC, SEC), SEC)
            u_ref[m, :, j, row_a, :] += ca_ref[own, :] * from_a[at, :]
            u_ref[m, :, j, row_b, :] += cb_ref[own, :] * from_b[at, :]

        each_rows(add)

    pl.when(parity[0] == 0)(lambda: rows(ROW - 1, 0))
    pl.when(parity[0] == 1)(lambda: rows(0, ROW - 1))
    fraction = frac_ref[...]
    for message, start in ((from_a, SEG), (from_b, SEG + 2 * CAP)):
        scale = cw_ref[pl.ds(start, CAP), :]
        for m in range(2):
            blocks = message[pl.ds(ROWS_MSG + m * SEG + CAP, CAP), :]
            term_ref[pl.ds(m * CAP, CAP), :] = terms(blocks, fraction, scale)
        scatter(src, start, CAP, u_ref, term_ref, CAP)


def section_adds(src, from_a, from_b, cw_ref, frac_ref, u_ref, term_ref):
    fraction = frac_ref[...]
    for message, start in ((from_a, 0), (from_b, 2 * SEG)):
        scale = cw_ref[pl.ds(start, SEG), :]
        for m in range(2):
            at = pl.ds(m * SEG, SEG)
            term_ref[at, :] = terms(message[at, :], fraction, scale)
        scatter(src, start, SEG, u_ref, term_ref, SEG)


def finish_kernel(src, wanted, parity, u_in, from_a, from_b, cw_ref, frac_ref, u_ref, a_ref, b_ref, term_ref):
    section_adds(src, from_a, from_b, cw_ref, frac_ref, u_ref, term_ref)
    pack_messages(wanted, parity, u_ref, a_ref, b_ref)


def last_kernel(src, u_in, from_a, from_b, cw_ref, frac_ref, u_ref, out_ref, term_ref, held_ref, sem):
    section_adds(src, from_a, from_b, cw_ref, frac_ref, u_ref, term_ref)

    def section(s, _):
        for m in range(2):
            for j in range(COLS):
                held_ref[m, s, :, lanes(j)] = u_ref[m, s, j]
            pltpu.make_async_copy(held_ref.at[m, s], out_ref.at[m, s], sem).start()
        return 0

    lax.fori_loop(0, SEC, section, 0)
    pltpu.make_async_copy(held_ref, out_ref, sem).wait()


def on_device(
    displacement,
    stiff_right,
    stiff_down,
    bilinear,
    match_source,
    match_target,
    match_count,
    match_weight,
):
    sec_count, tile_count = lax.axis_size("sec"), lax.axis_size("tile")
    sec, tile = lax.axis_index("sec"), lax.axis_index("tile")
    offset = jnp.arange(3, dtype=jnp.int32) - 1
    owner_sec, owner_tile = sec + offset, tile + offset
    valid = ((owner_sec >= 0) & (owner_sec < sec_count))[:, None] & (
        (owner_tile >= 0) & (owner_tile < tile_count)
    )[None, :]
    live = (jnp.arange(CAP, dtype=jnp.int32) < match_count[0][:, :, None]) & valid[:, :, None]

    def ordered(array):
        array = jnp.where(sec % 2 == 0, array[::-1], array)
        return jnp.where(tile % 2 == 0, array[:, ::-1], array)

    source = ordered(match_source[0]).reshape(-1)
    target = ordered(match_target[0])
    weight = ordered(jnp.where(live, match_weight[0], 0.0)).reshape(-1)
    parity = (tile % 2).astype(jnp.int32).reshape(1)
    keep = jnp.where(tile == tile_count - 1, 0.0, 1.0).astype(jnp.float32).reshape(1)
    fraction = jnp.where(jnp.arange(LANE) == LANE - 1, 0.0, bilinear).reshape(1, LANE)

    grid = (SEC, COLS, ROW, LANE)
    field = (2,) + grid
    rims = SEC * COLS
    asked_a, asked_b = exchange(target[0], target[2], "sec")
    kr, kd, dg, rim = kernel_call(setup_kernel, [vmem(*grid), vmem(*grid), vmem(*grid), vmem(rims, LANE)], 3, 2, cost=20_000_000)(
        source, weight, keep, stiff_right, stiff_down
    )
    (u,) = kernel_call(load_kernel, [vmem(*field)], 0, 1, cost=2_000_000)(displacement)

    def request(e):
        asked = jnp.concatenate([asked_a[e], target[1, e], asked_b[e]]).astype(jnp.float32)
        asked = jnp.pad(asked.reshape(1, SEG), ((0, 7), (0, LANE - SEG)))
        return jnp.concatenate([rim, asked], axis=0)

    got_a, got_b = exchange(request(0), request(2), "tile")
    wanted = jnp.concatenate([got_a[rims, :SEG], got_b[rims, :SEG]]).astype(jnp.int32)
    wanted_sec = jnp.concatenate([asked_a[1], asked_b[1]])
    cc, ca, cb, cw = kernel_call(
        coefficient_kernel, [vmem(*grid), vmem(rims, LANE), vmem(rims, LANE), vmem(9 * CAP, LANE)], 3, 4, cost=10_000_000
    )(source, weight, parity, dg, got_a, got_b, rim)

    messages = [vmem(T_MSG, LANE), vmem(T_MSG, LANE)]
    to_a, to_b = kernel_call(pack_kernel, messages, 2, 1, cost=1_000_000)(wanted, parity, u)
    local_target = target[1, 1]
    for step in range(ITERS):
        tile_a, tile_b = exchange(to_a, to_b, "tile")
        v, own_a, own_b = kernel_call(
            dense_kernel,
            [vmem(*field), vmem(2 * CAP, LANE), vmem(2 * CAP, LANE)],
            3,
            6,
            scratch=[vmem(2 * CAP, LANE)],
            cost=20_000_000,
        )(source, local_target, wanted_sec, u, kr, kd, cc, cw, fraction)
        sec_to_a, sec_to_b = kernel_call(relay_kernel, [vmem(2 * SEG, LANE)] * 2, 0, 4, cost=200_000)(
            tile_a, tile_b, own_a, own_b
        )
        sec_a, sec_b = exchange(sec_to_a, sec_to_b, "sec")
        (v,) = kernel_call(
            tile_kernel, [vmem(*field)], 2, 7, aliases={2: 0}, scratch=[vmem(2 * CAP, LANE)], cost=2_000_000
        )(source, parity, v, tile_a, tile_b, ca, cb, cw, fraction)
        if step + 1 < ITERS:
            u, to_a, to_b = kernel_call(
                finish_kernel, [vmem(*field)] + messages, 3, 5, aliases={3: 0}, scratch=[vmem(2 * SEG, LANE)], cost=2_000_000
            )(source, wanted, parity, v, sec_a, sec_b, cw, fraction)
        else:
            _, out = pl.pallas_call(
                last_kernel,
                out_shape=(vmem(*field), jax.ShapeDtypeStruct(displacement.shape, jnp.float32)),
                in_specs=[SM] + [VM] * 5,
                out_specs=(VM, pl.BlockSpec(memory_space=pl.ANY)),
                scratch_shapes=[vmem(2 * SEG, LANE), vmem(2, SEC, ROW, WID), pltpu.SemaphoreType.DMA],
                input_output_aliases={1: 0},
                compiler_params=pltpu.CompilerParams(vmem_limit_bytes=8 * 2**20),
            )(source, v, sec_a, sec_b, cw, fraction)
    return out


def solution(mesh):
    in_specs = (
        P(None, "sec", "tile", None),
        P("sec", "tile", None),
        P("sec", "tile", None),
        P(),
        P(("sec", "tile"), None, None, None),
        P(("sec", "tile"), None, None, None),
        P(("sec", "tile"), None, None),
        P(("sec", "tile"), None, None, None),
    )
    out_specs = P(None, "sec", "tile", None)
    return jax.shard_map(
        on_device, mesh=mesh, in_specs=in_specs, out_specs=out_specs, check_vma=False
    )
```

```python
import jax
import jax.numpy as jnp
from jax import lax
from jax.experimental import pallas as pl
from jax.experimental.pallas import tpu as pltpu
from jax.sharding import PartitionSpec as P

ITERS = 4
SEC = 16
ROW = 16
WID = 2048
LANE = 128
COLS = WID // LANE
CAP = 32
SEG = 3 * CAP
SECTION = COLS * ROW
PART = SEC * SECTION
PAD = 8
FIELD = 2 * PART + 2 * PAD
RIM = SEC * COLS
INNER = SEC - 2
ROW_MSG = 2 * INNER * COLS
EDGE = 2 * SEG
T_MSG = EDGE + 4 * COLS

VM = pl.BlockSpec(memory_space=pltpu.VMEM)
SM = pl.BlockSpec(memory_space=pltpu.SMEM)
HB = pl.BlockSpec(memory_space=pltpu.HBM)


def vmem(*shape):
    return pltpu.VMEM(shape, jnp.float32)


def kernel_call(body, outs, in_specs, aliases=None, scratch=(), cost=0, out_specs=None, limit=4):
    return pl.pallas_call(
        body,
        out_shape=tuple(outs),
        in_specs=in_specs,
        out_specs=out_specs or tuple(VM for _ in outs),
        scratch_shapes=list(scratch),
        input_output_aliases=aliases or {},
        compiler_params=pltpu.CompilerParams(vmem_limit_bytes=limit * 2**20),
        cost_estimate=pl.CostEstimate(flops=cost, bytes_accessed=cost, transcendentals=0),
        name=body.__name__,
    )


def pairing(axis, first):
    secs, tiles = lax.axis_size("sec"), lax.axis_size("tile")
    partner = {}
    for s in range(secs):
        for t in range(tiles):
            at, size = (t, tiles) if axis == "tile" else (s, secs)
            other = at + 1 if (at - first) % 2 == 0 else at - 1
            if axis == "tile":
                to = (s, other) if 0 <= other < size else (s ^ 1, t)
            else:
                to = (other, t) if 0 <= other < size else (s, t ^ 1)
            partner[s * tiles + t] = to[0] * tiles + to[1]
    return list(partner.items())


def exchange(to_a, to_b, axis):
    from_b = lax.ppermute(to_b, ("sec", "tile"), pairing(axis, 1))
    from_a = lax.ppermute(to_a, ("sec", "tile"), pairing(axis, 0))
    return from_a, from_b


def flat(block):
    return (block & 3840) | ((block & 15) << 4) | ((block >> 4) & 15)


def lanes(j):
    return slice(j * LANE, (j + 1) * LANE)


def iota(dim):
    return lax.broadcasted_iota(jnp.int32, (ROW, LANE), dim)


def loop(stop, body, step=1):
    def run(i, carry):
        body(i)
        return carry

    lax.fori_loop(0, stop, run, 0)


def live_slots(count, body):
    def group(i):
        for j in range(4):
            body(i * 4 + j)

    loop((count + 3) // 4, group)


def setup_kernel(
    first, after, keep, u_in, kr_in, kd_in, u_ref, kr_ref, kd_ref, dg_ref, a_ref, b_ref, kr_buf, kd_buf, sems
):
    lane, row = iota(1), iota(0)
    kept = keep[0]
    chunk = 4

    def copies(i):
        part = pl.ds(i * chunk, chunk)
        return (
            pltpu.make_async_copy(kr_in.at[part], kr_buf.at[part], sems.at[0, i]),
            pltpu.make_async_copy(kd_in.at[part], kd_buf.at[part], sems.at[1, i]),
        )

    for i in range(SEC // chunk):
        for copy in copies(i):
            copy.start()
    pack_rows(first, u_ref, a_ref, b_ref)
    kd_ref[pl.ds(0, PAD), :] = jnp.zeros((PAD, LANE), jnp.float32)

    def section(s):
        before = jnp.zeros((ROW, LANE), jnp.float32)
        for j in range(COLS):
            at = pl.multiple_of(s * SECTION + j * ROW, ROW)
            kr = kr_buf[s, :, lanes(j)]
            if j == COLS - 1:
                kr = jnp.where(lane == LANE - 1, 0.0, kr)
            kr_ref[pl.ds(at, ROW), :] = kr
            turned = pltpu.roll(kr, 1, 1)
            left = jnp.where(lane == 0, before, turned)
            before = turned
            kd = kd_buf[s, :, lanes(j)]
            inner = jnp.where(row == ROW - 1, 0.0, kd)
            kd_ref[pl.ds(at + PAD, ROW), :] = inner
            down = jnp.where(row == ROW - 1, kd * kept, kd)
            dg_ref[pl.ds(at, ROW), :] = 1.0 + kr + left + down + pltpu.roll(inner, 1, 0)

    for i in range(SEC // chunk):
        for copy in copies(i):
            copy.wait()
        loop(chunk, lambda s: section(s + i * chunk))


def row_at(m, s, row):
    return pl.ds(PAD + m * PART + s * SECTION + row, COLS, stride=ROW)


def cols_at(m, s):
    return pl.ds(pl.multiple_of((m * INNER + s - 1) * COLS, COLS), COLS)


def edge_at(m, q):
    return pl.ds(EDGE + (m * 2 + q) * COLS, COLS)


def first_row(first):
    return jnp.where(first[1] == 2, ROW - 1, 0)


def pack_rows(first, u_ref, a_ref, b_ref):
    row_a = first_row(first)

    def section(i):
        for m in range(2):
            a_ref[cols_at(m, i + 1), :] = u_ref[row_at(m, i + 1, row_a), :]
            b_ref[cols_at(m, i + 1), :] = u_ref[row_at(m, i + 1, ROW - 1 - row_a), :]

    loop(INNER, section)


def load_kernel(keep, field_in, kd_in, u_ref, rim_ref, buf, rim_buf, sems):
    chunk = 4

    def copies(i):
        part = pl.ds(i * chunk, chunk)
        return [pltpu.make_async_copy(field_in.at[m, part], buf.at[m, part], sems.at[m, i]) for m in range(2)]

    rim_copy = pltpu.make_async_copy(kd_in.at[:, ROW - 1], rim_buf, sems.at[2, 0])
    rim_copy.start()
    for i in range(SEC // chunk):
        for copy in copies(i):
            copy.start()
    zero = jnp.zeros((PAD, LANE), jnp.float32)
    u_ref[pl.ds(0, PAD), :] = zero
    u_ref[pl.ds(FIELD - PAD, PAD), :] = zero
    rim_copy.wait()
    kept = keep[0]
    for j in range(COLS):
        rim_ref[pl.ds(j, SEC, stride=COLS), :] = rim_buf[:, lanes(j)] * kept

    def section(s):
        for m in range(2):
            for j in range(COLS):
                at = pl.multiple_of(PAD + m * PART + s * SECTION + j * ROW, 8)
                u_ref[pl.ds(at, ROW), :] = buf[m, s, :, lanes(j)]

    for i in range(SEC // chunk):
        for copy in copies(i):
            copy.wait()
        loop(chunk, lambda s: section(s + i * chunk))


def diagonal_kernel(src, weight, count, dg_in, u_in, dg_ref, u_ref, cc_ref):
    for a in range(3):
        for e in range(3):
            number = count[0, a, e]

            def slot(k):
                at = pl.ds(src[0, a, e, k], 1)
                dg_ref[at, :] += jnp.where(k < number, weight[0, a, e, k], 0.0)

            live_slots(number, slot)

    def section(s):
        for j in range(COLS):
            at = pl.ds(pl.multiple_of(s * SECTION + j * ROW, ROW), ROW)
            cc_ref[at, :] = 0.8 / dg_ref[at, :]

    loop(SEC, section)


def coefficient_kernel(
    src, weight, count, first, dg_ref, got_a, got_b, rim, cc_in, u_in, cc_ref, u_ref, ca_ref, cb_ref, cw_ref
):
    even = first[1] == 2

    def rims(s):
        own = pl.ds(pl.multiple_of(s * COLS, COLS), COLS)
        top = pl.ds(s * SECTION, COLS, stride=ROW)
        upper = jnp.where(first[2] == 1, jnp.where(even, got_b[own, :], got_a[own, :]), 0.0)
        scale = 0.8 / (dg_ref[top, :] + upper)
        cc_ref[top, :] = scale
        upper = scale * upper
        lower = cc_ref[pl.ds(s * SECTION + ROW - 1, COLS, stride=ROW), :] * rim[own, :]
        ca_ref[own, :] = jnp.where(even, lower, upper)
        cb_ref[own, :] = jnp.where(even, upper, lower)

    loop(SEC, rims)
    for i, a in enumerate((first[0], 1, 2 - first[0])):
        for j, e in enumerate((first[1], 1, 2 - first[1])):
            number = count[0, a, e]

            def slot(k):
                value = cc_ref[pl.ds(src[0, a, e, k], 1), :]
                cw_ref[pl.ds((i * 3 + j) * CAP + k, 1), :] = value * jnp.where(k < number, weight[0, a, e, k], 0.0)

            live_slots(number, slot)


def pack_blocks(wanted, count, u_ref, msg_ref, at, stride):
    def group(i):
        for j in range(8):
            k = i * 8 + j
            block = wanted(k) + PAD
            for m in range(2):
                msg_ref[pl.ds(at + m * stride + k, 1), :] = u_ref[pl.ds(block + m * PART, 1), :]

    loop(count // 8, group)


def pack_messages(wanted, first, u_ref, a_ref, b_ref):
    row_a = first_row(first)
    pack_blocks(lambda k: wanted[k], SEG, u_ref, a_ref, 0, SEG)
    pack_blocks(lambda k: wanted[SEG + k], SEG, u_ref, b_ref, 0, SEG)
    for m in range(2):
        for q, s in enumerate((0, SEC - 1)):
            a_ref[edge_at(m, q), :] = u_ref[row_at(m, s, row_a), :]
            b_ref[edge_at(m, q), :] = u_ref[row_at(m, s, ROW - 1 - row_a), :]


def pack_kernel(wanted, first, u_in, u_ref, a_ref, b_ref):
    pack_messages(wanted, first, u_ref, a_ref, b_ref)


def terms(blocks, fraction, scale):
    return scale * (blocks + fraction * (pltpu.roll(blocks, LANE - 1, 1) - blocks))


def scatter(src, count, a, e, u_ref, term_ref, at, stride):
    def slot(k):
        block = src[0, a, e, k] + PAD
        places = [pl.ds(block + m * PART, 1) for m in range(2)]
        old = [u_ref[place, :] for place in places]
        add = [term_ref[pl.ds(at + m * stride + k, 1), :] for m in range(2)]
        for m in range(2):
            u_ref[places[m], :] = old[m] + add[m]

    live_slots(count[0, a, e], slot)


LOCAL = 4 * CAP


def dense_kernel(src, count, wanted_sec, u_in, kr_ref, kd_ref, cc_ref, cw_ref, frac_ref, u_ref, own_a, own_b, term_ref):
    lane = iota(1)
    zero = jnp.zeros((PAD, LANE), jnp.float32)
    u_ref[pl.ds(0, PAD), :] = zero
    u_ref[pl.ds(FIELD - PAD, PAD), :] = zero

    def section(s):
        def at(m, j, shift=0):
            return pl.ds(PAD + m * PART + s * SECTION + j * ROW + shift, ROW)

        here = [u_in[at(m, 0), :] for m in range(2)]
        here_turned = [pltpu.roll(x, LANE - 1, 1) for x in here]
        before = [jnp.zeros((ROW, LANE), jnp.float32)] * 2
        for j in range(COLS):
            own = pl.ds(s * SECTION + j * ROW, ROW)
            kr = kr_ref[own, :]
            kd = kd_ref[at(0, j), :]
            ku = kd_ref[at(0, j, -1), :]
            cc = cc_ref[own, :]
            for m in range(2):
                x = here[m]
                if j + 1 < COLS:
                    after = u_in[at(m, j + 1), :]
                    after_turned = pltpu.roll(after, LANE - 1, 1)
                    right = jnp.where(lane == LANE - 1, after_turned, here_turned[m])
                else:
                    after, after_turned, right = None, None, here_turned[m]
                turned = pltpu.roll(kr * x, 1, 1)
                total = x + kr * right + jnp.where(lane == 0, before[m], turned)
                total = total + kd * u_in[at(m, j, 1), :] + ku * u_in[at(m, j, -1), :]
                u_ref[at(m, j), :] = 0.2 * x + cc * total
                here[m], here_turned[m], before[m] = after, after_turned, turned

    loop(SEC, section)
    pack_blocks(lambda k: src[1, 1, 1, k], CAP, u_in, term_ref, 0, CAP)
    fraction = frac_ref[...]
    scale = cw_ref[pl.ds(LOCAL, CAP), :]
    for m in range(2):
        at = pl.ds(m * CAP, CAP)
        term_ref[at, :] = terms(term_ref[at, :], fraction, scale)
    scatter(src, count, 1, 1, u_ref, term_ref, 0, CAP)
    pack_blocks(lambda k: wanted_sec[k], CAP, u_in, own_a, 0, CAP)
    pack_blocks(lambda k: wanted_sec[CAP + k], CAP, u_in, own_b, 0, CAP)


def relay_kernel(from_a, from_b, own_a, own_b, a_ref, b_ref):
    for m in range(2):
        for out, own, seg in ((a_ref, own_a, 0), (b_ref, own_b, 2)):
            there = m * SEG + seg * CAP
            out[pl.ds(m * SEG, CAP), :] = from_a[pl.ds(there, CAP), :]
            out[pl.ds(m * SEG + CAP, CAP), :] = own[pl.ds(m * CAP, CAP), :]
            out[pl.ds(m * SEG + 2 * CAP, CAP), :] = from_b[pl.ds(there, CAP), :]


def tile_adds(src, count, first, from_a, from_b, rows_a, rows_b, ca_ref, cb_ref, cw_ref, frac_ref, u_ref, term_ref):
    row_a = first_row(first)

    def add(s, message_a, message_b, at):
        own = pl.ds(s * COLS, COLS)
        for m in range(2):
            u_ref[row_at(m, s, row_a), :] += ca_ref[own, :] * message_a[at(m), :]
            u_ref[row_at(m, s, ROW - 1 - row_a), :] += cb_ref[own, :] * message_b[at(m), :]

    loop(INNER, lambda i: add(i + 1, rows_a, rows_b, lambda m: cols_at(m, i + 1)))
    for q, s in enumerate((0, SEC - 1)):
        add(s, from_a, from_b, lambda m: edge_at(m, q))
    fraction = frac_ref[...]
    for message, start, e in ((from_a, SEG, first[1]), (from_b, SEG + 2 * CAP, 2 - first[1])):
        scale = cw_ref[pl.ds(start, CAP), :]
        for m in range(2):
            blocks = message[pl.ds(m * SEG + CAP, CAP), :]
            term_ref[pl.ds(m * CAP, CAP), :] = terms(blocks, fraction, scale)
        scatter(src, count, 1, e, u_ref, term_ref, 0, CAP)


def tile_kernel(
    src, count, first, u_in, from_a, from_b, rows_a, rows_b, ca_ref, cb_ref, cw_ref, frac_ref, u_ref, a_ref, b_ref, term_ref
):
    tile_adds(src, count, first, from_a, from_b, rows_a, rows_b, ca_ref, cb_ref, cw_ref, frac_ref, u_ref, term_ref)
    pack_rows(first, u_ref, a_ref, b_ref)


def last_tile_kernel(
    src, count, first, u_in, from_a, from_b, rows_a, rows_b, ca_ref, cb_ref, cw_ref, frac_ref, u_ref, term_ref
):
    tile_adds(src, count, first, from_a, from_b, rows_a, rows_b, ca_ref, cb_ref, cw_ref, frac_ref, u_ref, term_ref)


def section_adds(src, count, first, from_a, from_b, cw_ref, frac_ref, u_ref, term_ref):
    fraction = frac_ref[...]
    for message, start, a in ((from_a, 0, first[0]), (from_b, 2 * SEG, 2 - first[0])):
        scale = cw_ref[pl.ds(start, SEG), :]
        for m in range(2):
            at = pl.ds(m * SEG, SEG)
            term_ref[at, :] = terms(message[at, :], fraction, scale)
        for j, e in enumerate((first[1], 1, 2 - first[1])):
            scatter(src, count, a, e, u_ref, term_ref, j * CAP, SEG)


def finish_kernel(src, count, wanted, first, u_in, from_a, from_b, cw_ref, frac_ref, u_ref, a_ref, b_ref, term_ref):
    section_adds(src, count, first, from_a, from_b, cw_ref, frac_ref, u_ref, term_ref)
    pack_messages(wanted, first, u_ref, a_ref, b_ref)


def last_kernel(src, count, first, u_in, from_a, from_b, cw_ref, frac_ref, u_ref, out_ref, term_ref, held_ref, sem):
    section_adds(src, count, first, from_a, from_b, cw_ref, frac_ref, u_ref, term_ref)

    def section(s):
        for m in range(2):
            for j in range(COLS):
                at = pl.ds(pl.multiple_of(PAD + m * PART + s * SECTION + j * ROW, 8), ROW)
                held_ref[m, s, :, lanes(j)] = u_ref[at, :]
            pltpu.make_async_copy(held_ref.at[m, s], out_ref.at[m, s], sem).start()

    loop(SEC, section)
    pltpu.make_async_copy(held_ref, out_ref, sem).wait()


def on_device(
    displacement,
    stiff_right,
    stiff_down,
    bilinear,
    match_source,
    match_target,
    match_count,
    match_weight,
):
    tile_count = lax.axis_size("tile")
    sec, tile = lax.axis_index("sec"), lax.axis_index("tile")
    first = jnp.stack([2 - 2 * (sec % 2), 2 - 2 * (tile % 2), jnp.minimum(tile, 1)]).astype(jnp.int32)
    keep = jnp.where(tile == tile_count - 1, 0.0, 1.0).astype(jnp.float32).reshape(1)
    fraction = jnp.where(jnp.arange(LANE) == LANE - 1, 0.0, bilinear).reshape(1, LANE)

    displacement, stiff_right, stiff_down = (
        pltpu.with_memory_space_constraint(x, pltpu.HBM) for x in (displacement, stiff_right, stiff_down)
    )
    asked_a, asked_b = exchange(match_target, match_target, "sec")
    source = flat(jnp.concatenate([match_source, match_target]))
    asked_a, asked_b = flat(asked_a), flat(asked_b)
    rows = [vmem(ROW_MSG, LANE), vmem(ROW_MSG, LANE)]
    field = vmem(FIELD, LANE)
    u, rim = kernel_call(
        load_kernel,
        [field, vmem(RIM, LANE)],
        [SM, HB, HB],
        scratch=[vmem(2, SEC, ROW, WID), vmem(SEC, WID), pltpu.SemaphoreType.DMA((3, 4))],
        cost=6_000_000,
        limit=8,
    )(keep, displacement, stiff_down)

    def pick(array, a, e):
        return lax.dynamic_slice(array, (0, a, e, 0), (1, 1, 1, CAP)).reshape(CAP)

    def request(e):
        asked = jnp.concatenate([pick(asked_a, 2 - first[0], e), pick(source[1:], 1, e), pick(asked_b, first[0], e)])
        asked = jnp.pad(asked.astype(jnp.float32).reshape(1, SEG), ((0, 7), (0, LANE - SEG)))
        return jnp.concatenate([rim, asked], axis=0)

    got_a, got_b = exchange(request(first[1]), request(2 - first[1]), "tile")
    wanted = jnp.concatenate([got_a[RIM, :SEG], got_b[RIM, :SEG]]).astype(jnp.int32)
    wanted_sec = jnp.concatenate([pick(asked_a, 2 - first[0], 1), pick(asked_b, first[0], 1)])
    u, kr, kd, dg, rows_to_a, rows_to_b = kernel_call(
        setup_kernel,
        [field, vmem(PART, LANE), vmem(PART + 2 * PAD, LANE), vmem(PART, LANE), *rows],
        [SM, SM, SM, VM, HB, HB],
        aliases={3: 0},
        scratch=[vmem(SEC, ROW, WID), vmem(SEC, ROW, WID), pltpu.SemaphoreType.DMA((2, 4))],
        cost=6_000_000,
        limit=8,
    )(first, wanted_sec, keep, u, stiff_right, stiff_down)
    rows_a, rows_b = exchange(rows_to_a, rows_to_b, "tile")
    dg, u, cc = kernel_call(
        diagonal_kernel,
        [vmem(PART, LANE), field, vmem(PART, LANE)],
        [SM, SM, SM, VM, VM],
        aliases={3: 0, 4: 1},
        cost=4_000_000,
    )(source, match_weight, match_count, dg, u)
    messages = [vmem(T_MSG, LANE), vmem(T_MSG, LANE)]
    u, to_a, to_b = kernel_call(pack_kernel, [field, *messages], [SM, SM, VM], aliases={2: 0}, cost=1_000_000)(
        wanted, first, u
    )
    cc, u, ca, cb, cw = kernel_call(
        coefficient_kernel,
        [vmem(PART, LANE), field, vmem(RIM, LANE), vmem(RIM, LANE), vmem(9 * CAP, LANE)],
        [SM] * 4 + [VM] * 6,
        aliases={8: 0, 9: 1},
        cost=1_000_000,
    )(source, match_weight, match_count, first, dg, got_a, got_b, rim, cc, u)

    for step in range(ITERS):
        tile_a, tile_b = exchange(to_a, to_b, "tile")
        v, own_a, own_b = kernel_call(
            dense_kernel,
            [vmem(FIELD, LANE), vmem(2 * CAP, LANE), vmem(2 * CAP, LANE)],
            [SM] * 3 + [VM] * 6,
            scratch=[vmem(2 * CAP, LANE)],
            cost=20_000_000,
        )(source, match_count, wanted_sec, u, kr, kd, cc, cw, fraction)
        sec_to_a, sec_to_b = kernel_call(relay_kernel, [vmem(2 * SEG, LANE)] * 2, [VM] * 4, cost=200_000)(
            tile_a, tile_b, own_a, own_b
        )
        sec_a, sec_b = exchange(sec_to_a, sec_to_b, "sec")
        more = step + 1 < ITERS
        v, *rows_to = kernel_call(
            tile_kernel if more else last_tile_kernel,
            [vmem(FIELD, LANE)] + (rows if more else []),
            [SM] * 3 + [VM] * 9,
            aliases={3: 0},
            scratch=[vmem(2 * CAP, LANE)],
            cost=2_000_000,
        )(source, match_count, first, v, tile_a, tile_b, rows_a, rows_b, ca, cb, cw, fraction)
        if more:
            rows_a, rows_b = exchange(*rows_to, "tile")
        if step + 1 < ITERS:
            u, to_a, to_b = kernel_call(
                finish_kernel,
                [vmem(FIELD, LANE)] + messages,
                [SM] * 4 + [VM] * 5,
                aliases={4: 0},
                scratch=[vmem(2 * SEG, LANE)],
                cost=2_000_000,
            )(source, match_count, wanted, first, v, sec_a, sec_b, cw, fraction)
        else:
            _, out = kernel_call(
                last_kernel,
                [vmem(FIELD, LANE), jax.ShapeDtypeStruct(displacement.shape, jnp.float32)],
                [SM] * 3 + [VM] * 5,
                aliases={3: 0},
                scratch=[vmem(2 * SEG, LANE), vmem(2, SEC, ROW, WID), pltpu.SemaphoreType.DMA],
                cost=2_000_000,
                out_specs=(VM, HB),
                limit=8,
            )(source, match_count, first, v, sec_a, sec_b, cw, fraction)
    return out


def solution(mesh):
    in_specs = (
        P(None, "sec", "tile", None),
        P("sec", "tile", None),
        P("sec", "tile", None),
        P(),
        P(("sec", "tile"), None, None, None),
        P(("sec", "tile"), None, None, None),
        P(("sec", "tile"), None, None),
        P(("sec", "tile"), None, None, None),
    )
    out_specs = P(None, "sec", "tile", None)
    return jax.shard_map(
        on_device, mesh=mesh, in_specs=in_specs, out_specs=out_specs, check_vma=False
    )
```

```python
import jax
import jax.numpy as jnp
from jax import lax
from jax.experimental import pallas as pl
from jax.experimental.pallas import tpu as pltpu
from jax.sharding import PartitionSpec as P

ITERS = 4
SEC = 16
ROW = 16
WID = 2048
LANE = 128
COLS = WID // LANE
CAP = 32
SEG = 3 * CAP
SECTION = COLS * ROW
PART = SEC * SECTION
PAD = 8
FIELD = 2 * PART + 2 * PAD
RIM = SEC * COLS
INNER = SEC - 2
ROW_MSG = 2 * INNER * COLS
EDGE = 2 * SEG
T_MSG = EDGE + 4 * COLS

VM = pl.BlockSpec(memory_space=pltpu.VMEM)
SM = pl.BlockSpec(memory_space=pltpu.SMEM)
HB = pl.BlockSpec(memory_space=pltpu.HBM)


def vmem(*shape):
    return pltpu.VMEM(shape, jnp.float32)


def kernel_call(body, outs, in_specs, aliases=None, scratch=(), cost=0, out_specs=None, limit=4):
    return pl.pallas_call(
        body,
        out_shape=tuple(outs),
        in_specs=in_specs,
        out_specs=out_specs or tuple(VM for _ in outs),
        scratch_shapes=list(scratch),
        input_output_aliases=aliases or {},
        compiler_params=pltpu.CompilerParams(vmem_limit_bytes=limit * 2**20),
        cost_estimate=pl.CostEstimate(flops=cost, bytes_accessed=cost, transcendentals=0),
    )


def pairing(axis, first):
    secs, tiles = lax.axis_size("sec"), lax.axis_size("tile")
    partner = {}
    for s in range(secs):
        for t in range(tiles):
            at, size = (t, tiles) if axis == "tile" else (s, secs)
            other = at + 1 if (at - first) % 2 == 0 else at - 1
            if axis == "tile":
                to = (s, other) if 0 <= other < size else (s ^ 1, t)
            else:
                to = (other, t) if 0 <= other < size else (s, t ^ 1)
            partner[s * tiles + t] = to[0] * tiles + to[1]
    return list(partner.items())


def exchange(to_a, to_b, axis):
    from_b = lax.ppermute(to_b, ("sec", "tile"), pairing(axis, 1))
    from_a = lax.ppermute(to_a, ("sec", "tile"), pairing(axis, 0))
    return from_a, from_b


def flat(block):
    return (block & 3840) | ((block & 15) << 4) | ((block >> 4) & 15)


def lanes(j):
    return slice(j * LANE, (j + 1) * LANE)


def iota(dim):
    return lax.broadcasted_iota(jnp.int32, (ROW, LANE), dim)


def loop(stop, body):
    def run(i, carry):
        body(i)
        return carry

    lax.fori_loop(0, stop, run, 0)


def live_slots(count, body):
    def group(i):
        for j in range(4):
            body(i * 4 + j)

    loop((count + 3) // 4, group)


def setup_kernel(
    first, after, keep, u_in, kr_in, kd_in, u_ref, kr_ref, kd_ref, dg_ref, a_ref, b_ref, kr_buf, kd_buf, sems
):
    lane, row = iota(1), iota(0)
    kept = keep[0]
    chunk = 4

    def copies(i):
        part = pl.ds(i * chunk, chunk)
        return (
            pltpu.make_async_copy(kr_in.at[part], kr_buf.at[part], sems.at[0, i]),
            pltpu.make_async_copy(kd_in.at[part], kd_buf.at[part], sems.at[1, i]),
        )

    for i in range(SEC // chunk):
        for copy in copies(i):
            copy.start()
    pack_rows(first, u_ref, a_ref, b_ref)
    kd_ref[pl.ds(0, PAD), :] = jnp.zeros((PAD, LANE), jnp.float32)

    def section(s):
        before = jnp.zeros((ROW, LANE), jnp.float32)
        for j in range(COLS):
            at = pl.multiple_of(s * SECTION + j * ROW, ROW)
            kr = kr_buf[s, :, lanes(j)]
            if j == COLS - 1:
                kr = jnp.where(lane == LANE - 1, 0.0, kr)
            kr_ref[pl.ds(at, ROW), :] = kr
            turned = pltpu.roll(kr, 1, 1)
            left = jnp.where(lane == 0, before, turned)
            before = turned
            kd = kd_buf[s, :, lanes(j)]
            inner = jnp.where(row == ROW - 1, 0.0, kd)
            kd_ref[pl.ds(at + PAD, ROW), :] = inner
            down = jnp.where(row == ROW - 1, kd * kept, kd)
            dg_ref[pl.ds(at, ROW), :] = 1.0 + kr + left + down + pltpu.roll(inner, 1, 0)

    for i in range(SEC // chunk):
        for copy in copies(i):
            copy.wait()
        loop(chunk, lambda s: section(s + i * chunk))


def row_at(m, s, row):
    return pl.ds(PAD + m * PART + s * SECTION + row, COLS, stride=ROW)


def cols_at(m, s):
    return pl.ds(pl.multiple_of((m * INNER + s - 1) * COLS, COLS), COLS)


def edge_at(m, q):
    return pl.ds(EDGE + (m * 2 + q) * COLS, COLS)


def first_row(first):
    return jnp.where(first[1] == 2, ROW - 1, 0)


def pack_rows(first, u_ref, a_ref, b_ref):
    row_a = first_row(first)

    def section(i):
        for m in range(2):
            a_ref[cols_at(m, i + 1), :] = u_ref[row_at(m, i + 1, row_a), :]
            b_ref[cols_at(m, i + 1), :] = u_ref[row_at(m, i + 1, ROW - 1 - row_a), :]

    loop(INNER, section)


def load_kernel(keep, field_in, kd_in, u_ref, rim_ref, buf, rim_buf, sems):
    chunk = 4

    def copies(i):
        part = pl.ds(i * chunk, chunk)
        return [pltpu.make_async_copy(field_in.at[m, part], buf.at[m, part], sems.at[m, i]) for m in range(2)]

    rim_copy = pltpu.make_async_copy(kd_in.at[:, ROW - 1], rim_buf, sems.at[2, 0])
    rim_copy.start()
    for i in range(SEC // chunk):
        for copy in copies(i):
            copy.start()
    zero = jnp.zeros((PAD, LANE), jnp.float32)
    u_ref[pl.ds(0, PAD), :] = zero
    u_ref[pl.ds(FIELD - PAD, PAD), :] = zero
    rim_copy.wait()
    kept = keep[0]
    for j in range(COLS):
        rim_ref[pl.ds(j, SEC, stride=COLS), :] = rim_buf[:, lanes(j)] * kept

    def section(s):
        for m in range(2):
            for j in range(COLS):
                at = pl.multiple_of(PAD + m * PART + s * SECTION + j * ROW, 8)
                u_ref[pl.ds(at, ROW), :] = buf[m, s, :, lanes(j)]

    for i in range(SEC // chunk):
        for copy in copies(i):
            copy.wait()
        loop(chunk, lambda s: section(s + i * chunk))


def diagonal_kernel(src, weight, count, dg_in, u_in, dg_ref, u_ref, cc_ref):
    for a in range(3):
        for e in range(3):
            number = count[0, a, e]

            def slot(k):
                at = pl.ds(src[0, a, e, k], 1)
                dg_ref[at, :] += jnp.where(k < number, weight[0, a, e, k], 0.0)

            live_slots(number, slot)

    def section(s):
        for j in range(COLS):
            at = pl.ds(pl.multiple_of(s * SECTION + j * ROW, ROW), ROW)
            cc_ref[at, :] = 0.8 / dg_ref[at, :]

    loop(SEC, section)


def coefficient_kernel(
    src, weight, count, first, dg_ref, got_a, got_b, rim, cc_in, u_in, cc_ref, u_ref, ca_ref, cb_ref, cw_ref
):
    even = first[1] == 2

    def rims(s):
        own = pl.ds(pl.multiple_of(s * COLS, COLS), COLS)
        top = pl.ds(s * SECTION, COLS, stride=ROW)
        upper = jnp.where(first[2] == 1, jnp.where(even, got_b[own, :], got_a[own, :]), 0.0)
        scale = 0.8 / (dg_ref[top, :] + upper)
        cc_ref[top, :] = scale
        upper = scale * upper
        lower = cc_ref[pl.ds(s * SECTION + ROW - 1, COLS, stride=ROW), :] * rim[own, :]
        ca_ref[own, :] = jnp.where(even, lower, upper)
        cb_ref[own, :] = jnp.where(even, upper, lower)

    loop(SEC, rims)
    for i, a in enumerate((first[0], 1, 2 - first[0])):
        for j, e in enumerate((first[1], 1, 2 - first[1])):
            number = count[0, a, e]

            def slot(k):
                value = cc_ref[pl.ds(src[0, a, e, k], 1), :]
                cw_ref[pl.ds((i * 3 + j) * CAP + k, 1), :] = value * jnp.where(k < number, weight[0, a, e, k], 0.0)

            live_slots(number, slot)


def pack_blocks(wanted, count, u_ref, msg_ref, at, stride):
    def group(i):
        for j in range(8):
            k = i * 8 + j
            block = wanted(k) + PAD
            for m in range(2):
                msg_ref[pl.ds(at + m * stride + k, 1), :] = u_ref[pl.ds(block + m * PART, 1), :]

    loop(count // 8, group)


def pack_messages(wanted, first, u_ref, a_ref, b_ref):
    row_a = first_row(first)
    pack_blocks(lambda k: wanted[k], SEG, u_ref, a_ref, 0, SEG)
    pack_blocks(lambda k: wanted[SEG + k], SEG, u_ref, b_ref, 0, SEG)
    for m in range(2):
        for q, s in enumerate((0, SEC - 1)):
            a_ref[edge_at(m, q), :] = u_ref[row_at(m, s, row_a), :]
            b_ref[edge_at(m, q), :] = u_ref[row_at(m, s, ROW - 1 - row_a), :]


def pack_kernel(wanted, first, u_in, u_ref, a_ref, b_ref):
    pack_messages(wanted, first, u_ref, a_ref, b_ref)


def terms(blocks, fraction, scale):
    return scale * (blocks + fraction * (pltpu.roll(blocks, LANE - 1, 1) - blocks))


def scatter(src, count, a, e, u_ref, term_ref, at, stride):
    def slot(k):
        block = src[0, a, e, k] + PAD
        places = [pl.ds(block + m * PART, 1) for m in range(2)]
        old = [u_ref[place, :] for place in places]
        add = [term_ref[pl.ds(at + m * stride + k, 1), :] for m in range(2)]
        for m in range(2):
            u_ref[places[m], :] = old[m] + add[m]

    live_slots(count[0, a, e], slot)


LOCAL = 4 * CAP


def dense_kernel(src, count, wanted_sec, u_in, kr_ref, kd_ref, cc_ref, cw_ref, frac_ref, u_ref, own_a, own_b, term_ref):
    lane = iota(1)
    zero = jnp.zeros((PAD, LANE), jnp.float32)
    u_ref[pl.ds(0, PAD), :] = zero
    u_ref[pl.ds(FIELD - PAD, PAD), :] = zero

    def section(s):
        def at(m, j, shift=0):
            return pl.ds(PAD + m * PART + s * SECTION + j * ROW + shift, ROW)

        here = [u_in[at(m, 0), :] for m in range(2)]
        here_turned = [pltpu.roll(x, LANE - 1, 1) for x in here]
        before = [jnp.zeros((ROW, LANE), jnp.float32)] * 2
        for j in range(COLS):
            own = pl.ds(s * SECTION + j * ROW, ROW)
            kr = kr_ref[own, :]
            kd = kd_ref[at(0, j), :]
            ku = kd_ref[at(0, j, -1), :]
            cc = cc_ref[own, :]
            for m in range(2):
                x = here[m]
                if j + 1 < COLS:
                    after = u_in[at(m, j + 1), :]
                    after_turned = pltpu.roll(after, LANE - 1, 1)
                    right = jnp.where(lane == LANE - 1, after_turned, here_turned[m])
                else:
                    after, after_turned, right = None, None, here_turned[m]
                turned = pltpu.roll(kr * x, 1, 1)
                total = x + kr * right + jnp.where(lane == 0, before[m], turned)
                total = total + kd * u_in[at(m, j, 1), :] + ku * u_in[at(m, j, -1), :]
                u_ref[at(m, j), :] = 0.2 * x + cc * total
                here[m], here_turned[m], before[m] = after, after_turned, turned

    loop(SEC, section)
    pack_blocks(lambda k: src[1, 1, 1, k], CAP, u_in, term_ref, 0, CAP)
    fraction = frac_ref[...]
    scale = cw_ref[pl.ds(LOCAL, CAP), :]
    for m in range(2):
        at = pl.ds(m * CAP, CAP)
        term_ref[at, :] = terms(term_ref[at, :], fraction, scale)
    scatter(src, count, 1, 1, u_ref, term_ref, 0, CAP)
    pack_blocks(lambda k: wanted_sec[k], CAP, u_in, own_a, 0, CAP)
    pack_blocks(lambda k: wanted_sec[CAP + k], CAP, u_in, own_b, 0, CAP)


def relay_kernel(from_a, from_b, own_a, own_b, a_ref, b_ref):
    for m in range(2):
        for out, own, seg in ((a_ref, own_a, 0), (b_ref, own_b, 2)):
            there = m * SEG + seg * CAP
            out[pl.ds(m * SEG, CAP), :] = from_a[pl.ds(there, CAP), :]
            out[pl.ds(m * SEG + CAP, CAP), :] = own[pl.ds(m * CAP, CAP), :]
            out[pl.ds(m * SEG + 2 * CAP, CAP), :] = from_b[pl.ds(there, CAP), :]


def tile_adds(
    src, count, first, from_a, from_b, rows_a, rows_b, ca_ref, cb_ref, cw_ref, frac_ref, u_ref, term_ref, a_ref=None, b_ref=None
):
    row_a = first_row(first)
    fraction = frac_ref[...]
    for message, start, e in ((from_a, SEG, first[1]), (from_b, SEG + 2 * CAP, 2 - first[1])):
        scale = cw_ref[pl.ds(start, CAP), :]
        for m in range(2):
            blocks = message[pl.ds(m * SEG + CAP, CAP), :]
            term_ref[pl.ds(m * CAP, CAP), :] = terms(blocks, fraction, scale)
        scatter(src, count, 1, e, u_ref, term_ref, 0, CAP)

    def add(s, message_a, message_b, at, to_a, to_b):
        own = pl.ds(s * COLS, COLS)
        for m in range(2):
            for row, scale, message, to in ((row_a, ca_ref, message_a, to_a), (ROW - 1 - row_a, cb_ref, message_b, to_b)):
                value = u_ref[row_at(m, s, row), :] + scale[own, :] * message[at(m), :]
                u_ref[row_at(m, s, row), :] = value
                if to is not None:
                    to[at(m), :] = value

    loop(INNER, lambda i: add(i + 1, rows_a, rows_b, lambda m: cols_at(m, i + 1), a_ref, b_ref))
    for q, s in enumerate((0, SEC - 1)):
        add(s, from_a, from_b, lambda m: edge_at(m, q), None, None)


def tile_kernel(
    src, count, first, u_in, from_a, from_b, rows_a, rows_b, ca_ref, cb_ref, cw_ref, frac_ref, u_ref, a_ref, b_ref, term_ref
):
    tile_adds(
        src, count, first, from_a, from_b, rows_a, rows_b, ca_ref, cb_ref, cw_ref, frac_ref, u_ref, term_ref, a_ref, b_ref
    )


def write_section(s, u_ref, held_ref, out_ref, sem):
    for m in range(2):
        for j in range(COLS):
            at = pl.ds(pl.multiple_of(PAD + m * PART + s * SECTION + j * ROW, 8), ROW)
            held_ref[m, s, :, lanes(j)] = u_ref[at, :]
        pltpu.make_async_copy(held_ref.at[m, s], out_ref.at[m, s], sem).start()


def last_tile_kernel(
    src, count, first, u_in, from_a, from_b, rows_a, rows_b, ca_ref, cb_ref, cw_ref, frac_ref, u_ref, out_ref, term_ref, held_ref, sem
):
    tile_adds(src, count, first, from_a, from_b, rows_a, rows_b, ca_ref, cb_ref, cw_ref, frac_ref, u_ref, term_ref)
    loop(INNER, lambda i: write_section(i + 1, u_ref, held_ref, out_ref, sem))
    inner = (slice(None), pl.ds(1, INNER))
    pltpu.make_async_copy(held_ref.at[inner], out_ref.at[inner], sem).wait()


def section_adds(src, count, first, from_a, from_b, cw_ref, frac_ref, u_ref, term_ref):
    fraction = frac_ref[...]
    for message, start, a in ((from_a, 0, first[0]), (from_b, 2 * SEG, 2 - first[0])):
        scale = cw_ref[pl.ds(start, SEG), :]
        for m in range(2):
            at = pl.ds(m * SEG, SEG)
            term_ref[at, :] = terms(message[at, :], fraction, scale)
        for j, e in enumerate((first[1], 1, 2 - first[1])):
            scatter(src, count, a, e, u_ref, term_ref, j * CAP, SEG)


def finish_kernel(src, count, wanted, first, u_in, from_a, from_b, cw_ref, frac_ref, u_ref, a_ref, b_ref, term_ref):
    section_adds(src, count, first, from_a, from_b, cw_ref, frac_ref, u_ref, term_ref)
    pack_messages(wanted, first, u_ref, a_ref, b_ref)


def last_kernel(src, count, first, u_in, out_in, from_a, from_b, cw_ref, frac_ref, u_ref, out_ref, term_ref, held_ref, sem):
    section_adds(src, count, first, from_a, from_b, cw_ref, frac_ref, u_ref, term_ref)
    for q, s in enumerate((0, SEC - 1)):
        for m in range(2):
            for j in range(COLS):
                held_ref[q, m, :, lanes(j)] = u_ref[pl.ds(PAD + m * PART + s * SECTION + j * ROW, ROW), :]
            pltpu.make_async_copy(held_ref.at[q, m], out_ref.at[m, s], sem.at[q, m]).start()
    for q, s in enumerate((0, SEC - 1)):
        for m in range(2):
            pltpu.make_async_copy(held_ref.at[q, m], out_ref.at[m, s], sem.at[q, m]).wait()


def on_device(
    displacement,
    stiff_right,
    stiff_down,
    bilinear,
    match_source,
    match_target,
    match_count,
    match_weight,
):
    tile_count = lax.axis_size("tile")
    sec, tile = lax.axis_index("sec"), lax.axis_index("tile")
    first = jnp.stack([2 - 2 * (sec % 2), 2 - 2 * (tile % 2), jnp.minimum(tile, 1)]).astype(jnp.int32)
    keep = jnp.where(tile == tile_count - 1, 0.0, 1.0).astype(jnp.float32).reshape(1)
    fraction = jnp.where(jnp.arange(LANE) == LANE - 1, 0.0, bilinear).reshape(1, LANE)

    displacement, stiff_right, stiff_down = (
        pltpu.with_memory_space_constraint(x, pltpu.HBM) for x in (displacement, stiff_right, stiff_down)
    )
    asked_a, asked_b = exchange(match_target, match_target, "sec")
    source = flat(jnp.concatenate([match_source, match_target]))
    asked_a, asked_b = flat(asked_a), flat(asked_b)
    rows = [vmem(ROW_MSG, LANE), vmem(ROW_MSG, LANE)]
    field = vmem(FIELD, LANE)
    u, rim = kernel_call(
        load_kernel,
        [field, vmem(RIM, LANE)],
        [SM, HB, HB],
        scratch=[vmem(2, SEC, ROW, WID), vmem(SEC, WID), pltpu.SemaphoreType.DMA((3, 4))],
        cost=6_000_000,
        limit=8,
    )(keep, displacement, stiff_down)

    def pick(array, a, e):
        return lax.dynamic_slice(array, (0, a, e, 0), (1, 1, 1, CAP)).reshape(CAP)

    def request(e):
        asked = jnp.concatenate([pick(asked_a, 2 - first[0], e), pick(source[1:], 1, e), pick(asked_b, first[0], e)])
        asked = jnp.pad(asked.astype(jnp.float32).reshape(1, SEG), ((0, 7), (0, LANE - SEG)))
        return jnp.concatenate([rim, asked], axis=0)

    got_a, got_b = exchange(request(first[1]), request(2 - first[1]), "tile")
    wanted = jnp.concatenate([got_a[RIM, :SEG], got_b[RIM, :SEG]]).astype(jnp.int32)
    wanted_sec = jnp.concatenate([pick(asked_a, 2 - first[0], 1), pick(asked_b, first[0], 1)])
    u, kr, kd, dg, rows_to_a, rows_to_b = kernel_call(
        setup_kernel,
        [field, vmem(PART, LANE), vmem(PART + 2 * PAD, LANE), vmem(PART, LANE), *rows],
        [SM, SM, SM, VM, HB, HB],
        aliases={3: 0},
        scratch=[vmem(SEC, ROW, WID), vmem(SEC, ROW, WID), pltpu.SemaphoreType.DMA((2, 4))],
        cost=6_000_000,
        limit=8,
    )(first, wanted_sec, keep, u, stiff_right, stiff_down)
    rows_a, rows_b = exchange(rows_to_a, rows_to_b, "tile")
    dg, u, cc = kernel_call(
        diagonal_kernel,
        [vmem(PART, LANE), field, vmem(PART, LANE)],
        [SM, SM, SM, VM, VM],
        aliases={3: 0, 4: 1},
        cost=4_000_000,
    )(source, match_weight, match_count, dg, u)
    messages = [vmem(T_MSG, LANE), vmem(T_MSG, LANE)]
    u, to_a, to_b = kernel_call(pack_kernel, [field, *messages], [SM, SM, VM], aliases={2: 0}, cost=1_000_000)(
        wanted, first, u
    )
    cc, u, ca, cb, cw = kernel_call(
        coefficient_kernel,
        [vmem(PART, LANE), field, vmem(RIM, LANE), vmem(RIM, LANE), vmem(9 * CAP, LANE)],
        [SM] * 4 + [VM] * 6,
        aliases={8: 0, 9: 1},
        cost=1_000_000,
    )(source, match_weight, match_count, first, dg, got_a, got_b, rim, cc, u)

    whole = jax.ShapeDtypeStruct(displacement.shape, jnp.float32)
    for step in range(ITERS):
        tile_a, tile_b = exchange(to_a, to_b, "tile")
        v, own_a, own_b = kernel_call(
            dense_kernel,
            [field, vmem(2 * CAP, LANE), vmem(2 * CAP, LANE)],
            [SM] * 3 + [VM] * 6,
            scratch=[vmem(2 * CAP, LANE)],
            cost=20_000_000,
        )(source, match_count, wanted_sec, u, kr, kd, cc, cw, fraction)
        sec_to_a, sec_to_b = kernel_call(relay_kernel, [vmem(2 * SEG, LANE)] * 2, [VM] * 4, cost=200_000)(
            tile_a, tile_b, own_a, own_b
        )
        sec_a, sec_b = exchange(sec_to_a, sec_to_b, "sec")
        received = (tile_a, tile_b, rows_a, rows_b, ca, cb, cw, fraction)
        if step + 1 < ITERS:
            v, *rows_to = kernel_call(
                tile_kernel,
                [field] + rows,
                [SM] * 3 + [VM] * 9,
                aliases={3: 0},
                scratch=[vmem(2 * CAP, LANE)],
                cost=2_000_000,
            )(source, match_count, first, v, *received)
            rows_a, rows_b = exchange(*rows_to, "tile")
            u, to_a, to_b = kernel_call(
                finish_kernel,
                [field] + messages,
                [SM] * 4 + [VM] * 5,
                aliases={4: 0},
                scratch=[vmem(2 * SEG, LANE)],
                cost=2_000_000,
            )(source, match_count, wanted, first, v, sec_a, sec_b, cw, fraction)
        else:
            v, out = kernel_call(
                last_tile_kernel,
                [field, whole],
                [SM] * 3 + [VM] * 9,
                aliases={3: 0},
                scratch=[vmem(2 * CAP, LANE), vmem(2, SEC, ROW, WID), pltpu.SemaphoreType.DMA],
                cost=4_000_000,
                out_specs=(VM, HB),
                limit=8,
            )(source, match_count, first, v, *received)
            _, out = kernel_call(
                last_kernel,
                [field, whole],
                [SM] * 3 + [VM, HB] + [VM] * 4,
                aliases={3: 0, 4: 1},
                scratch=[vmem(2 * SEG, LANE), vmem(2, 2, ROW, WID), pltpu.SemaphoreType.DMA((2, 2))],
                cost=2_000_000,
                out_specs=(VM, HB),
            )(source, match_count, first, v, out, sec_a, sec_b, cw, fraction)
    return out


def solution(mesh):
    in_specs = (
        P(None, "sec", "tile", None),
        P("sec", "tile", None),
        P("sec", "tile", None),
        P(),
        P(("sec", "tile"), None, None, None),
        P(("sec", "tile"), None, None, None),
        P(("sec", "tile"), None, None),
        P(("sec", "tile"), None, None, None),
    )
    out_specs = P(None, "sec", "tile", None)
    return jax.shard_map(
        on_device, mesh=mesh, in_specs=in_specs, out_specs=out_specs, check_vma=False
    )
```

```python
import jax
import jax.numpy as jnp
from jax import lax
from jax.experimental import pallas as pl
from jax.experimental.pallas import tpu as pltpu
from jax.sharding import PartitionSpec as P

ITERS = 4
SEC = 16
ROW = 16
WID = 2048
LANE = 128
COLS = WID // LANE
CAP = 32
SEG = 3 * CAP
SECTION = COLS * ROW
PART = SEC * SECTION
PAD = 8
FIELD = 2 * PART + 2 * PAD
RIM = SEC * COLS
INNER = SEC - 2
ROW_MSG = 2 * INNER * COLS
EDGE = 2 * SEG
T_MSG = EDGE + 4 * COLS

VM = pl.BlockSpec(memory_space=pltpu.VMEM)
SM = pl.BlockSpec(memory_space=pltpu.SMEM)
HB = pl.BlockSpec(memory_space=pltpu.HBM)
ANY = pl.BlockSpec(memory_space=pl.ANY)


def vmem(*shape):
    return pltpu.VMEM(shape, jnp.float32)


def kernel_call(body, outs, in_specs, aliases=None, scratch=(), cost=0, out_specs=None, limit=4):
    return pl.pallas_call(
        body,
        out_shape=tuple(outs),
        in_specs=in_specs,
        out_specs=out_specs or tuple(VM for _ in outs),
        scratch_shapes=list(scratch),
        input_output_aliases=aliases or {},
        compiler_params=pltpu.CompilerParams(vmem_limit_bytes=limit * 2**20),
        cost_estimate=pl.CostEstimate(flops=cost, bytes_accessed=cost, transcendentals=0),
    )


def pairing(axis, first):
    secs, tiles = lax.axis_size("sec"), lax.axis_size("tile")
    partner = {}
    for s in range(secs):
        for t in range(tiles):
            at, size = (t, tiles) if axis == "tile" else (s, secs)
            other = at + 1 if (at - first) % 2 == 0 else at - 1
            if axis == "tile":
                to = (s, other) if 0 <= other < size else (s ^ 1, t)
            else:
                to = (other, t) if 0 <= other < size else (s, t ^ 1)
            partner[s * tiles + t] = to[0] * tiles + to[1]
    return list(partner.items())


def exchange(to_a, to_b, axis):
    from_b = lax.ppermute(to_b, ("sec", "tile"), pairing(axis, 1))
    from_a = lax.ppermute(to_a, ("sec", "tile"), pairing(axis, 0))
    return from_a, from_b


def flat(block):
    return (block & 3840) | ((block & 15) << 4) | ((block >> 4) & 15)


def lanes(j):
    return slice(j * LANE, (j + 1) * LANE)


def iota(dim):
    return lax.broadcasted_iota(jnp.int32, (ROW, LANE), dim)


def loop(stop, body):
    def run(i, carry):
        body(i)
        return carry

    lax.fori_loop(0, stop, run, 0)


def live_slots(count, body):
    def group(i):
        for j in range(8):
            body(i * 8 + j)

    loop((count + 7) // 8, group)


def slots_at(a, e):
    return (a * 3 + e) * CAP


GROUP = 8


def grouped_adds(block, count, term, ref, parts):
    def group(i):
        for j in range(GROUP):
            place = block(i * GROUP + j)
            old = [ref[pl.ds(place + part, 1), :] for part in parts]
            for m, part in enumerate(parts):
                ref[pl.ds(place + part, 1), :] = old[m] + term(i * GROUP + j, m)

    loop((count + GROUP - 1) // GROUP, group)


def setup_kernel(
    first, after, keep, u_in, kr_in, kd_in, u_ref, kr_ref, kd_ref, dg_ref, a_ref, b_ref, kr_buf, kd_buf, sems
):
    lane, row = iota(1), iota(0)
    kept = keep[0]
    chunk = 4

    def copies(i):
        part = pl.ds(i * chunk, chunk)
        return (
            pltpu.make_async_copy(kr_in.at[part], kr_buf.at[part], sems.at[0, i]),
            pltpu.make_async_copy(kd_in.at[part], kd_buf.at[part], sems.at[1, i]),
        )

    for i in range(SEC // chunk):
        for copy in copies(i):
            copy.start()
    pack_rows(first, u_ref, a_ref, b_ref)
    kd_ref[pl.ds(0, PAD), :] = jnp.zeros((PAD, LANE), jnp.float32)

    def section(s):
        before = jnp.zeros((ROW, LANE), jnp.float32)
        for j in range(COLS):
            at = pl.multiple_of(s * SECTION + j * ROW, ROW)
            kr = kr_buf[s, :, lanes(j)]
            if j == COLS - 1:
                kr = jnp.where(lane == LANE - 1, 0.0, kr)
            kr_ref[pl.ds(at, ROW), :] = kr
            turned = pltpu.roll(kr, 1, 1)
            left = jnp.where(lane == 0, before, turned)
            before = turned
            kd = kd_buf[s, :, lanes(j)]
            inner = jnp.where(row == ROW - 1, 0.0, kd)
            kd_ref[pl.ds(at + PAD, ROW), :] = inner
            down = jnp.where(row == ROW - 1, kd * kept, kd)
            dg_ref[pl.ds(at, ROW), :] = 1.0 + kr + left + down + pltpu.roll(inner, 1, 0)

    for i in range(SEC // chunk):
        for copy in copies(i):
            copy.wait()
        loop(chunk, lambda s: section(s + i * chunk))


def row_at(m, s, row):
    return pl.ds(PAD + m * PART + s * SECTION + row, COLS, stride=ROW)


def cols_at(m, s):
    return pl.ds(pl.multiple_of((m * INNER + s - 1) * COLS, COLS), COLS)


def edge_at(m, q):
    return pl.ds(EDGE + (m * 2 + q) * COLS, COLS)


def first_row(first):
    return jnp.where(first[1] == 2, ROW - 1, 0)


def pack_rows(first, u_ref, a_ref, b_ref):
    row_a = first_row(first)

    def section(i):
        for m in range(2):
            a_ref[cols_at(m, i + 1), :] = u_ref[row_at(m, i + 1, row_a), :]
            b_ref[cols_at(m, i + 1), :] = u_ref[row_at(m, i + 1, ROW - 1 - row_a), :]

    loop(INNER, section)


def load_kernel(keep, src, weight, field_in, kd_in, u_ref, rim_ref, buf, rim_buf, sems):
    chunk = 4

    def copies(i):
        part = pl.ds(i * chunk, chunk)
        return [pltpu.make_async_copy(field_in.at[m, part], buf.at[m, part], sems.at[m, i]) for m in range(2)]

    rim_copy = pltpu.make_async_copy(kd_in.at[:, ROW - 1], rim_buf, sems.at[2, 0])
    rim_copy.start()
    for i in range(SEC // chunk):
        for copy in copies(i):
            copy.start()
    zero = jnp.zeros((PAD, LANE), jnp.float32)
    u_ref[pl.ds(0, PAD), :] = zero
    u_ref[pl.ds(FIELD - PAD, PAD), :] = zero
    rim_copy.wait()
    kept = keep[0]
    for j in range(COLS):
        rim_ref[pl.ds(j, SEC, stride=COLS), :] = rim_buf[:, lanes(j)] * kept

    def section(s):
        for m in range(2):
            for j in range(COLS):
                at = pl.multiple_of(PAD + m * PART + s * SECTION + j * ROW, 8)
                u_ref[pl.ds(at, ROW), :] = buf[m, s, :, lanes(j)]

    for i in range(SEC // chunk):
        for copy in copies(i):
            copy.wait()
        loop(chunk, lambda s: section(s + i * chunk))


def diagonal_kernel(src, weight, count, dg_in, u_in, dg_ref, u_ref, cc_ref):
    for a in range(3):
        for e in range(3):
            number, base = count[0, a, e], slots_at(a, e)

            def term(k, m):
                return jnp.full((1, LANE), jnp.where(k < number, weight[base + k], 0.0), jnp.float32)

            grouped_adds(lambda k: src[base + k], number, term, dg_ref, (0,))

    def section(s):
        for j in range(COLS):
            at = pl.ds(pl.multiple_of(s * SECTION + j * ROW, ROW), ROW)
            cc_ref[at, :] = 0.8 / dg_ref[at, :]

    loop(SEC, section)


def coefficient_kernel(
    src, weight, count, first, dg_ref, got_a, got_b, rim, cc_in, u_in, cc_ref, u_ref, ca_ref, cb_ref, cw_ref
):
    even = first[1] == 2

    def rims(s):
        own = pl.ds(pl.multiple_of(s * COLS, COLS), COLS)
        top = pl.ds(s * SECTION, COLS, stride=ROW)
        upper = jnp.where(first[2] == 1, jnp.where(even, got_b[own, :], got_a[own, :]), 0.0)
        scale = 0.8 / (dg_ref[top, :] + upper)
        cc_ref[top, :] = scale
        upper = scale * upper
        lower = cc_ref[pl.ds(s * SECTION + ROW - 1, COLS, stride=ROW), :] * rim[own, :]
        ca_ref[own, :] = jnp.where(even, lower, upper)
        cb_ref[own, :] = jnp.where(even, upper, lower)

    loop(SEC, rims)
    for i, a in enumerate((first[0], 1, 2 - first[0])):
        for j, e in enumerate((first[1], 1, 2 - first[1])):
            number, base = count[0, a, e], slots_at(a, e)

            def slot(k):
                value = cc_ref[pl.ds(src[base + k], 1), :]
                cw_ref[pl.ds((i * 3 + j) * CAP + k, 1), :] = value * jnp.where(k < number, weight[base + k], 0.0)

            live_slots(number, slot)


def pack_blocks(wanted, count, u_ref, msg_ref, at, stride):
    def group(i):
        for j in range(8):
            k = i * 8 + j
            block = wanted(k) + PAD
            for m in range(2):
                msg_ref[pl.ds(at + m * stride + k, 1), :] = u_ref[pl.ds(block + m * PART, 1), :]

    loop(count // 8, group)


def pack_messages(wanted, first, u_ref, a_ref, b_ref):
    row_a = first_row(first)
    pack_blocks(lambda k: wanted[k], SEG, u_ref, a_ref, 0, SEG)
    pack_blocks(lambda k: wanted[SEG + k], SEG, u_ref, b_ref, 0, SEG)
    for m in range(2):
        for q, s in enumerate((0, SEC - 1)):
            a_ref[edge_at(m, q), :] = u_ref[row_at(m, s, row_a), :]
            b_ref[edge_at(m, q), :] = u_ref[row_at(m, s, ROW - 1 - row_a), :]


def pack_kernel(wanted, first, u_in, u_ref, a_ref, b_ref):
    pack_messages(wanted, first, u_ref, a_ref, b_ref)


def terms(blocks, fraction, scale):
    return scale * (blocks + fraction * (pltpu.roll(blocks, LANE - 1, 1) - blocks))


def scatter(src, count, a, e, u_ref, term_ref, at, stride):
    def term(k, m):
        return term_ref[pl.ds(at + m * stride + k, 1), :]

    base = slots_at(a, e)
    grouped_adds(lambda k: src[base + k] + PAD, count[0, a, e], term, u_ref, (0, PART))


LOCAL = 4 * CAP


def dense_kernel(src, count, wanted_sec, u_in, kr_ref, kd_ref, cc_ref, cw_ref, frac_ref, u_ref, own_a, own_b, term_ref):
    lane = iota(1)
    zero = jnp.zeros((PAD, LANE), jnp.float32)
    u_ref[pl.ds(0, PAD), :] = zero
    u_ref[pl.ds(FIELD - PAD, PAD), :] = zero

    def section(s):
        def at(m, j, shift=0):
            return pl.ds(PAD + m * PART + s * SECTION + j * ROW + shift, ROW)

        here = [u_in[at(m, 0), :] for m in range(2)]
        here_turned = [pltpu.roll(x, LANE - 1, 1) for x in here]
        before = [jnp.zeros((ROW, LANE), jnp.float32)] * 2
        for j in range(COLS):
            own = pl.ds(s * SECTION + j * ROW, ROW)
            kr = kr_ref[own, :]
            kd = kd_ref[at(0, j), :]
            ku = kd_ref[at(0, j, -1), :]
            cc = cc_ref[own, :]
            for m in range(2):
                x = here[m]
                if j + 1 < COLS:
                    after = u_in[at(m, j + 1), :]
                    after_turned = pltpu.roll(after, LANE - 1, 1)
                    right = jnp.where(lane == LANE - 1, after_turned, here_turned[m])
                else:
                    after, after_turned, right = None, None, here_turned[m]
                turned = pltpu.roll(kr * x, 1, 1)
                total = x + kr * right + jnp.where(lane == 0, before[m], turned)
                total = total + kd * u_in[at(m, j, 1), :] + ku * u_in[at(m, j, -1), :]
                u_ref[at(m, j), :] = 0.2 * x + cc * total
                here[m], here_turned[m], before[m] = after, after_turned, turned

    loop(SEC, section)
    pack_blocks(lambda k: src[(9 + 4) * CAP + k], CAP, u_in, term_ref, 0, CAP)
    fraction = frac_ref[...]
    scale = cw_ref[pl.ds(LOCAL, CAP), :]
    for m in range(2):
        at = pl.ds(m * CAP, CAP)
        term_ref[at, :] = terms(term_ref[at, :], fraction, scale)
    scatter(src, count, 1, 1, u_ref, term_ref, 0, CAP)
    pack_blocks(lambda k: wanted_sec[k], CAP, u_in, own_a, 0, CAP)
    pack_blocks(lambda k: wanted_sec[CAP + k], CAP, u_in, own_b, 0, CAP)


def relay_kernel(from_a, from_b, own_a, own_b, a_ref, b_ref):
    for m in range(2):
        for out, own, seg in ((a_ref, own_a, 0), (b_ref, own_b, 2)):
            there = m * SEG + seg * CAP
            out[pl.ds(m * SEG, CAP), :] = from_a[pl.ds(there, CAP), :]
            out[pl.ds(m * SEG + CAP, CAP), :] = own[pl.ds(m * CAP, CAP), :]
            out[pl.ds(m * SEG + 2 * CAP, CAP), :] = from_b[pl.ds(there, CAP), :]


def tile_adds(
    src, count, first, from_a, from_b, rows_a, rows_b, ca_ref, cb_ref, cw_ref, frac_ref, u_ref, term_ref, a_ref=None, b_ref=None
):
    row_a = first_row(first)
    fraction = frac_ref[...]
    for message, start, e in ((from_a, SEG, first[1]), (from_b, SEG + 2 * CAP, 2 - first[1])):
        scale = cw_ref[pl.ds(start, CAP), :]
        for m in range(2):
            blocks = message[pl.ds(m * SEG + CAP, CAP), :]
            term_ref[pl.ds(m * CAP, CAP), :] = terms(blocks, fraction, scale)
        scatter(src, count, 1, e, u_ref, term_ref, 0, CAP)

    def add(s, message_a, message_b, at, to_a, to_b):
        own = pl.ds(s * COLS, COLS)
        for m in range(2):
            for row, scale, message, to in ((row_a, ca_ref, message_a, to_a), (ROW - 1 - row_a, cb_ref, message_b, to_b)):
                value = u_ref[row_at(m, s, row), :] + scale[own, :] * message[at(m), :]
                u_ref[row_at(m, s, row), :] = value
                if to is not None:
                    to[at(m), :] = value

    loop(INNER, lambda i: add(i + 1, rows_a, rows_b, lambda m: cols_at(m, i + 1), a_ref, b_ref))
    for q, s in enumerate((0, SEC - 1)):
        add(s, from_a, from_b, lambda m: edge_at(m, q), None, None)


def tile_kernel(
    src, count, first, u_in, from_a, from_b, rows_a, rows_b, ca_ref, cb_ref, cw_ref, frac_ref, u_ref, a_ref, b_ref, term_ref
):
    tile_adds(
        src, count, first, from_a, from_b, rows_a, rows_b, ca_ref, cb_ref, cw_ref, frac_ref, u_ref, term_ref, a_ref, b_ref
    )


def write_section(s, u_ref, held_ref, out_ref, sem):
    for m in range(2):
        for j in range(COLS):
            at = pl.ds(pl.multiple_of(PAD + m * PART + s * SECTION + j * ROW, 8), ROW)
            held_ref[m, s, :, lanes(j)] = u_ref[at, :]
        pltpu.make_async_copy(held_ref.at[m, s], out_ref.at[m, s], sem).start()


def last_tile_kernel(
    src, count, first, u_in, from_a, from_b, rows_a, rows_b, ca_ref, cb_ref, cw_ref, frac_ref, u_ref, out_ref, term_ref, held_ref, sem
):
    tile_adds(src, count, first, from_a, from_b, rows_a, rows_b, ca_ref, cb_ref, cw_ref, frac_ref, u_ref, term_ref)
    loop(INNER, lambda i: write_section(i + 1, u_ref, held_ref, out_ref, sem))
    inner = (slice(None), pl.ds(1, INNER))
    pltpu.make_async_copy(held_ref.at[inner], out_ref.at[inner], sem).wait()


def section_adds(src, count, first, from_a, from_b, cw_ref, frac_ref, u_ref, term_ref):
    fraction = frac_ref[...]
    for message, start, a in ((from_a, 0, first[0]), (from_b, 2 * SEG, 2 - first[0])):
        scale = cw_ref[pl.ds(start, SEG), :]
        for m in range(2):
            at = pl.ds(m * SEG, SEG)
            term_ref[at, :] = terms(message[at, :], fraction, scale)
        for j, e in enumerate((first[1], 1, 2 - first[1])):
            scatter(src, count, a, e, u_ref, term_ref, j * CAP, SEG)


def finish_kernel(src, count, wanted, first, u_in, from_a, from_b, cw_ref, frac_ref, u_ref, a_ref, b_ref, term_ref):
    section_adds(src, count, first, from_a, from_b, cw_ref, frac_ref, u_ref, term_ref)
    pack_messages(wanted, first, u_ref, a_ref, b_ref)


def last_kernel(src, count, first, u_in, out_in, from_a, from_b, cw_ref, frac_ref, u_ref, out_ref, term_ref, held_ref, sem):
    section_adds(src, count, first, from_a, from_b, cw_ref, frac_ref, u_ref, term_ref)
    for q, s in enumerate((0, SEC - 1)):
        for m in range(2):
            for j in range(COLS):
                held_ref[q, m, :, lanes(j)] = u_ref[pl.ds(PAD + m * PART + s * SECTION + j * ROW, ROW), :]
            pltpu.make_async_copy(held_ref.at[q, m], out_ref.at[m, s], sem.at[q, m]).start()
    for q, s in enumerate((0, SEC - 1)):
        for m in range(2):
            pltpu.make_async_copy(held_ref.at[q, m], out_ref.at[m, s], sem.at[q, m]).wait()


def on_device(
    displacement,
    stiff_right,
    stiff_down,
    bilinear,
    match_source,
    match_target,
    match_count,
    match_weight,
):
    tile_count = lax.axis_size("tile")
    sec, tile = lax.axis_index("sec"), lax.axis_index("tile")
    first = jnp.stack([2 - 2 * (sec % 2), 2 - 2 * (tile % 2), jnp.minimum(tile, 1)]).astype(jnp.int32)
    keep = jnp.where(tile == tile_count - 1, 0.0, 1.0).astype(jnp.float32).reshape(1)
    fraction = jnp.where(jnp.arange(LANE) == LANE - 1, 0.0, bilinear).reshape(1, LANE)

    displacement, stiff_right, stiff_down = (
        pltpu.with_memory_space_constraint(x, pltpu.HBM) for x in (displacement, stiff_right, stiff_down)
    )
    asked_a, asked_b = exchange(match_target, match_target, "sec")
    which = lax.broadcasted_iota(jnp.int32, (2,) + match_source.shape[1:], 0)
    ids = flat(jnp.where(which == 0, match_source, match_target))
    source, weight = ids.reshape(-1), match_weight.reshape(-1)
    asked_a, asked_b = flat(asked_a), flat(asked_b)
    rows = [vmem(ROW_MSG, LANE), vmem(ROW_MSG, LANE)]
    field = vmem(FIELD, LANE)
    u, rim = kernel_call(
        load_kernel,
        [field, vmem(RIM, LANE)],
        [SM, ANY, ANY, HB, HB],
        scratch=[vmem(2, SEC, ROW, WID), vmem(SEC, WID), pltpu.SemaphoreType.DMA((3, 4))],
        cost=6_000_000,
        limit=8,
    )(keep, source, weight, displacement, stiff_down)

    def pick(array, a, e):
        return lax.dynamic_slice(array, (0, a, e, 0), (1, 1, 1, CAP)).reshape(CAP)

    def request(e):
        asked = jnp.concatenate([pick(asked_a, 2 - first[0], e), pick(ids[1:], 1, e), pick(asked_b, first[0], e)])
        asked = jnp.pad(asked.astype(jnp.float32).reshape(1, SEG), ((0, 7), (0, LANE - SEG)))
        return jnp.concatenate([rim, asked], axis=0)

    got_a, got_b = exchange(request(first[1]), request(2 - first[1]), "tile")
    wanted = jnp.concatenate([got_a[RIM, :SEG], got_b[RIM, :SEG]]).astype(jnp.int32)
    wanted_sec = jnp.concatenate([pick(asked_a, 2 - first[0], 1), pick(asked_b, first[0], 1)])
    u, kr, kd, dg, rows_to_a, rows_to_b = kernel_call(
        setup_kernel,
        [field, vmem(PART, LANE), vmem(PART + 2 * PAD, LANE), vmem(PART, LANE), *rows],
        [SM, SM, SM, VM, HB, HB],
        aliases={3: 0},
        scratch=[vmem(SEC, ROW, WID), vmem(SEC, ROW, WID), pltpu.SemaphoreType.DMA((2, 4))],
        cost=6_000_000,
        limit=8,
    )(first, wanted_sec, keep, u, stiff_right, stiff_down)
    rows_a, rows_b = exchange(rows_to_a, rows_to_b, "tile")
    dg, u, cc = kernel_call(
        diagonal_kernel,
        [vmem(PART, LANE), field, vmem(PART, LANE)],
        [SM, SM, SM, VM, VM],
        aliases={3: 0, 4: 1},
        cost=4_000_000,
    )(source, weight, match_count, dg, u)
    messages = [vmem(T_MSG, LANE), vmem(T_MSG, LANE)]
    u, to_a, to_b = kernel_call(pack_kernel, [field, *messages], [SM, SM, VM], aliases={2: 0}, cost=1_000_000)(
        wanted, first, u
    )
    cc, u, ca, cb, cw = kernel_call(
        coefficient_kernel,
        [vmem(PART, LANE), field, vmem(RIM, LANE), vmem(RIM, LANE), vmem(9 * CAP, LANE)],
        [SM] * 4 + [VM] * 6,
        aliases={8: 0, 9: 1},
        cost=1_000_000,
    )(source, weight, match_count, first, dg, got_a, got_b, rim, cc, u)

    whole = jax.ShapeDtypeStruct(displacement.shape, jnp.float32)
    for step in range(ITERS):
        tile_a, tile_b = exchange(to_a, to_b, "tile")
        v, own_a, own_b = kernel_call(
            dense_kernel,
            [field, vmem(2 * CAP, LANE), vmem(2 * CAP, LANE)],
            [SM] * 3 + [VM] * 6,
            scratch=[vmem(2 * CAP, LANE)],
            cost=20_000_000,
        )(source, match_count, wanted_sec, u, kr, kd, cc, cw, fraction)
        sec_to_a, sec_to_b = kernel_call(relay_kernel, [vmem(2 * SEG, LANE)] * 2, [VM] * 4, cost=200_000)(
            tile_a, tile_b, own_a, own_b
        )
        sec_a, sec_b = exchange(sec_to_a, sec_to_b, "sec")
        received = (tile_a, tile_b, rows_a, rows_b, ca, cb, cw, fraction)
        if step + 1 < ITERS:
            v, *rows_to = kernel_call(
                tile_kernel,
                [field] + rows,
                [SM] * 3 + [VM] * 9,
                aliases={3: 0},
                scratch=[vmem(2 * CAP, LANE)],
                cost=2_000_000,
            )(source, match_count, first, v, *received)
            rows_a, rows_b = exchange(*rows_to, "tile")
            u, to_a, to_b = kernel_call(
                finish_kernel,
                [field] + messages,
                [SM] * 4 + [VM] * 5,
                aliases={4: 0},
                scratch=[vmem(2 * SEG, LANE)],
                cost=2_000_000,
            )(source, match_count, wanted, first, v, sec_a, sec_b, cw, fraction)
        else:
            v, out = kernel_call(
                last_tile_kernel,
                [field, whole],
                [SM] * 3 + [VM] * 9,
                aliases={3: 0},
                scratch=[vmem(2 * CAP, LANE), vmem(2, SEC, ROW, WID), pltpu.SemaphoreType.DMA],
                cost=4_000_000,
                out_specs=(VM, HB),
                limit=8,
            )(source, match_count, first, v, *received)
            _, out = kernel_call(
                last_kernel,
                [field, whole],
                [SM] * 3 + [VM, HB] + [VM] * 4,
                aliases={3: 0, 4: 1},
                scratch=[vmem(2 * SEG, LANE), vmem(2, 2, ROW, WID), pltpu.SemaphoreType.DMA((2, 2))],
                cost=2_000_000,
                out_specs=(VM, HB),
            )(source, match_count, first, v, out, sec_a, sec_b, cw, fraction)
    return out


def solution(mesh):
    in_specs = (
        P(None, "sec", "tile", None),
        P("sec", "tile", None),
        P("sec", "tile", None),
        P(),
        P(("sec", "tile"), None, None, None),
        P(("sec", "tile"), None, None, None),
        P(("sec", "tile"), None, None),
        P(("sec", "tile"), None, None, None),
    )
    out_specs = P(None, "sec", "tile", None)
    return jax.shard_map(
        on_device, mesh=mesh, in_specs=in_specs, out_specs=out_specs, check_vma=False
    )
```

```python
import jax
import jax.numpy as jnp
from jax import lax
from jax.experimental import pallas as pl
from jax.experimental.pallas import tpu as pltpu
from jax.sharding import PartitionSpec as P

ITERS = 4
SEC = 16
ROW = 16
WID = 2048
LANE = 128
COLS = WID // LANE
CAP = 32
SEG = 3 * CAP
SECTION = COLS * ROW
PART = SEC * SECTION
PAD = 8
FIELD = 2 * PART + 2 * PAD
RIM = SEC * COLS
INNER = SEC - 2
ROW_MSG = 2 * INNER * COLS
EDGE = 2 * SEG
T_MSG = EDGE + 4 * COLS

VM = pl.BlockSpec(memory_space=pltpu.VMEM)
SM = pl.BlockSpec(memory_space=pltpu.SMEM)
HB = pl.BlockSpec(memory_space=pltpu.HBM)
ANY = pl.BlockSpec(memory_space=pl.ANY)


def vmem(*shape):
    return pltpu.VMEM(shape, jnp.float32)


def kernel_call(body, outs, in_specs, aliases=None, scratch=(), cost=0, out_specs=None, limit=4):
    return pl.pallas_call(
        body,
        out_shape=tuple(outs),
        in_specs=in_specs,
        out_specs=out_specs or tuple(VM for _ in outs),
        scratch_shapes=list(scratch),
        input_output_aliases=aliases or {},
        compiler_params=pltpu.CompilerParams(vmem_limit_bytes=limit * 2**20),
        cost_estimate=pl.CostEstimate(flops=cost, bytes_accessed=cost, transcendentals=0),
    )


def pairing(axis, first):
    secs, tiles = lax.axis_size("sec"), lax.axis_size("tile")
    partner = {}
    for s in range(secs):
        for t in range(tiles):
            at, size = (t, tiles) if axis == "tile" else (s, secs)
            other = at + 1 if (at - first) % 2 == 0 else at - 1
            if axis == "tile":
                to = (s, other) if 0 <= other < size else (s ^ 1, t)
            else:
                to = (other, t) if 0 <= other < size else (s, t ^ 1)
            partner[s * tiles + t] = to[0] * tiles + to[1]
    return list(partner.items())


def exchange(to_a, to_b, axis):
    from_b = lax.ppermute(to_b, ("sec", "tile"), pairing(axis, 1))
    from_a = lax.ppermute(to_a, ("sec", "tile"), pairing(axis, 0))
    return from_a, from_b


def flat(block):
    return (block & 3840) | ((block & 15) << 4) | ((block >> 4) & 15)


def lanes(j):
    return slice(j * LANE, (j + 1) * LANE)


def iota(dim):
    return lax.broadcasted_iota(jnp.int32, (ROW, LANE), dim)


def loop(stop, body):
    def run(i, carry):
        body(i)
        return carry

    lax.fori_loop(0, stop, run, 0)


def live_slots(count, body):
    def group(i):
        for j in range(8):
            body(i * 8 + j)

    loop((count + 7) // 8, group)


def slots_at(a, e):
    return (a * 3 + e) * CAP


GROUP = 8


def grouped_adds(block, count, term, ref, parts):
    def group(i):
        for j in range(GROUP):
            place = block(i * GROUP + j)
            old = [ref[pl.ds(place + part, 1), :] for part in parts]
            for m, part in enumerate(parts):
                ref[pl.ds(place + part, 1), :] = old[m] + term(i * GROUP + j, m)

    loop((count + GROUP - 1) // GROUP, group)


def setup_kernel(
    first, after, keep, u_in, kr_in, kd_in, u_ref, kr_ref, kd_ref, dg_ref, a_ref, b_ref, kr_buf, kd_buf, sems
):
    lane, row = iota(1), iota(0)
    kept = keep[0]
    chunk = 4

    def copies(i):
        part = pl.ds(i * chunk, chunk)
        return (
            pltpu.make_async_copy(kr_in.at[part], kr_buf.at[part], sems.at[0, i]),
            pltpu.make_async_copy(kd_in.at[part], kd_buf.at[part], sems.at[1, i]),
        )

    for i in range(SEC // chunk):
        for copy in copies(i):
            copy.start()
    pack_rows(first, u_ref, a_ref, b_ref)
    kd_ref[pl.ds(0, PAD), :] = jnp.zeros((PAD, LANE), jnp.float32)

    def section(s):
        before = jnp.zeros((ROW, LANE), jnp.float32)
        for j in range(COLS):
            at = pl.multiple_of(s * SECTION + j * ROW, ROW)
            kr = kr_buf[s, :, lanes(j)]
            if j == COLS - 1:
                kr = jnp.where(lane == LANE - 1, 0.0, kr)
            kr_ref[pl.ds(at, ROW), :] = kr
            turned = pltpu.roll(kr, 1, 1)
            left = jnp.where(lane == 0, before, turned)
            before = turned
            kd = kd_buf[s, :, lanes(j)]
            inner = jnp.where(row == ROW - 1, 0.0, kd)
            kd_ref[pl.ds(at + PAD, ROW), :] = inner
            down = jnp.where(row == ROW - 1, kd * kept, kd)
            dg_ref[pl.ds(at, ROW), :] = 1.0 + kr + left + down + pltpu.roll(inner, 1, 0)

    for i in range(SEC // chunk):
        for copy in copies(i):
            copy.wait()
        loop(chunk, lambda s: section(s + i * chunk))


def row_at(m, s, row):
    return pl.ds(PAD + m * PART + s * SECTION + row, COLS, stride=ROW)


def cols_at(m, s):
    return pl.ds(pl.multiple_of((m * INNER + s - 1) * COLS, COLS), COLS)


def edge_at(m, q):
    return pl.ds(EDGE + (m * 2 + q) * COLS, COLS)


def first_row(first):
    return jnp.where(first[1] == 2, ROW - 1, 0)


def pack_rows(first, u_ref, a_ref, b_ref):
    row_a = first_row(first)

    def section(i):
        for m in range(2):
            a_ref[cols_at(m, i + 1), :] = u_ref[row_at(m, i + 1, row_a), :]
            b_ref[cols_at(m, i + 1), :] = u_ref[row_at(m, i + 1, ROW - 1 - row_a), :]

    loop(INNER, section)


def load_kernel(keep, src, field_in, kd_in, u_ref, rim_ref, buf, rim_buf, sems):
    chunk = 4

    def copies(i):
        part = pl.ds(i * chunk, chunk)
        return [pltpu.make_async_copy(field_in.at[m, part], buf.at[m, part], sems.at[m, i]) for m in range(2)]

    rim_copy = pltpu.make_async_copy(kd_in.at[:, ROW - 1], rim_buf, sems.at[2, 0])
    rim_copy.start()
    for i in range(SEC // chunk):
        for copy in copies(i):
            copy.start()
    zero = jnp.zeros((PAD, LANE), jnp.float32)
    u_ref[pl.ds(0, PAD), :] = zero
    u_ref[pl.ds(FIELD - PAD, PAD), :] = zero
    rim_copy.wait()
    kept = keep[0]
    for j in range(COLS):
        rim_ref[pl.ds(j, SEC, stride=COLS), :] = rim_buf[:, lanes(j)] * kept

    def section(s):
        for m in range(2):
            for j in range(COLS):
                at = pl.multiple_of(PAD + m * PART + s * SECTION + j * ROW, 8)
                u_ref[pl.ds(at, ROW), :] = buf[m, s, :, lanes(j)]

    for i in range(SEC // chunk):
        for copy in copies(i):
            copy.wait()
        loop(chunk, lambda s: section(s + i * chunk))


def diagonal_kernel(src, weight, count, dg_in, u_in, dg_ref, u_ref, cc_ref):
    for a in range(3):
        for e in range(3):
            number, base = count[0, a, e], slots_at(a, e)

            def term(k, m):
                return jnp.full((1, LANE), jnp.where(k < number, weight[0, a, e, k], 0.0), jnp.float32)

            grouped_adds(lambda k: src[base + k], number, term, dg_ref, (0,))

    def section(s):
        for j in range(COLS):
            at = pl.ds(pl.multiple_of(s * SECTION + j * ROW, ROW), ROW)
            cc_ref[at, :] = 0.8 / dg_ref[at, :]

    loop(SEC, section)


def coefficient_kernel(
    src, weight, count, first, dg_ref, got_a, got_b, rim, cc_in, u_in, cc_ref, u_ref, ca_ref, cb_ref, cw_ref
):
    even = first[1] == 2

    def rims(s):
        own = pl.ds(pl.multiple_of(s * COLS, COLS), COLS)
        top = pl.ds(s * SECTION, COLS, stride=ROW)
        upper = jnp.where(first[2] == 1, jnp.where(even, got_b[own, :], got_a[own, :]), 0.0)
        scale = 0.8 / (dg_ref[top, :] + upper)
        cc_ref[top, :] = scale
        upper = scale * upper
        lower = cc_ref[pl.ds(s * SECTION + ROW - 1, COLS, stride=ROW), :] * rim[own, :]
        ca_ref[own, :] = jnp.where(even, lower, upper)
        cb_ref[own, :] = jnp.where(even, upper, lower)

    loop(SEC, rims)
    for i, a in enumerate((first[0], 1, 2 - first[0])):
        for j, e in enumerate((first[1], 1, 2 - first[1])):
            number, base = count[0, a, e], slots_at(a, e)

            def slot(k):
                value = cc_ref[pl.ds(src[base + k], 1), :]
                cw_ref[pl.ds((i * 3 + j) * CAP + k, 1), :] = value * jnp.where(k < number, weight[0, a, e, k], 0.0)

            live_slots(number, slot)


def pack_blocks(wanted, count, u_ref, msg_ref, at, stride):
    def group(i):
        for j in range(8):
            k = i * 8 + j
            block = wanted(k) + PAD
            for m in range(2):
                msg_ref[pl.ds(at + m * stride + k, 1), :] = u_ref[pl.ds(block + m * PART, 1), :]

    loop(count // 8, group)


def pack_messages(wanted, first, u_ref, a_ref, b_ref):
    row_a = first_row(first)
    pack_blocks(lambda k: wanted[k], SEG, u_ref, a_ref, 0, SEG)
    pack_blocks(lambda k: wanted[SEG + k], SEG, u_ref, b_ref, 0, SEG)
    for m in range(2):
        for q, s in enumerate((0, SEC - 1)):
            a_ref[edge_at(m, q), :] = u_ref[row_at(m, s, row_a), :]
            b_ref[edge_at(m, q), :] = u_ref[row_at(m, s, ROW - 1 - row_a), :]


def pack_kernel(wanted, first, u_in, u_ref, a_ref, b_ref):
    pack_messages(wanted, first, u_ref, a_ref, b_ref)


def terms(blocks, fraction, scale):
    return scale * (blocks + fraction * (pltpu.roll(blocks, LANE - 1, 1) - blocks))


def scatter(src, count, a, e, u_ref, term_ref, at, stride):
    def term(k, m):
        return term_ref[pl.ds(at + m * stride + k, 1), :]

    base = slots_at(a, e)
    grouped_adds(lambda k: src[base + k] + PAD, count[0, a, e], term, u_ref, (0, PART))


LOCAL = 4 * CAP


def dense_kernel(src, count, wanted_sec, u_in, kr_ref, kd_ref, cc_ref, cw_ref, frac_ref, u_ref, own_a, own_b, term_ref):
    lane = iota(1)
    zero = jnp.zeros((PAD, LANE), jnp.float32)
    u_ref[pl.ds(0, PAD), :] = zero
    u_ref[pl.ds(FIELD - PAD, PAD), :] = zero

    def section(s):
        def at(m, j, shift=0):
            return pl.ds(PAD + m * PART + s * SECTION + j * ROW + shift, ROW)

        here = [u_in[at(m, 0), :] for m in range(2)]
        here_turned = [pltpu.roll(x, LANE - 1, 1) for x in here]
        before = [jnp.zeros((ROW, LANE), jnp.float32)] * 2
        for j in range(COLS):
            own = pl.ds(s * SECTION + j * ROW, ROW)
            kr = kr_ref[own, :]
            kd = kd_ref[at(0, j), :]
            ku = kd_ref[at(0, j, -1), :]
            cc = cc_ref[own, :]
            for m in range(2):
                x = here[m]
                if j + 1 < COLS:
                    after = u_in[at(m, j + 1), :]
                    after_turned = pltpu.roll(after, LANE - 1, 1)
                    right = jnp.where(lane == LANE - 1, after_turned, here_turned[m])
                else:
                    after, after_turned, right = None, None, here_turned[m]
                turned = pltpu.roll(kr * x, 1, 1)
                total = x + kr * right + jnp.where(lane == 0, before[m], turned)
                total = total + kd * u_in[at(m, j, 1), :] + ku * u_in[at(m, j, -1), :]
                u_ref[at(m, j), :] = 0.2 * x + cc * total
                here[m], here_turned[m], before[m] = after, after_turned, turned

    loop(SEC, section)
    pack_blocks(lambda k: src[(9 + 4) * CAP + k], CAP, u_in, term_ref, 0, CAP)
    fraction = frac_ref[...]
    scale = cw_ref[pl.ds(LOCAL, CAP), :]
    for m in range(2):
        at = pl.ds(m * CAP, CAP)
        term_ref[at, :] = terms(term_ref[at, :], fraction, scale)
    scatter(src, count, 1, 1, u_ref, term_ref, 0, CAP)
    pack_blocks(lambda k: wanted_sec[k], CAP, u_in, own_a, 0, CAP)
    pack_blocks(lambda k: wanted_sec[CAP + k], CAP, u_in, own_b, 0, CAP)


def relay_kernel(from_a, from_b, own_a, own_b, a_ref, b_ref):
    for m in range(2):
        for out, own, seg in ((a_ref, own_a, 0), (b_ref, own_b, 2)):
            there = m * SEG + seg * CAP
            out[pl.ds(m * SEG, CAP), :] = from_a[pl.ds(there, CAP), :]
            out[pl.ds(m * SEG + CAP, CAP), :] = own[pl.ds(m * CAP, CAP), :]
            out[pl.ds(m * SEG + 2 * CAP, CAP), :] = from_b[pl.ds(there, CAP), :]


def tile_adds(
    src, count, first, from_a, from_b, rows_a, rows_b, ca_ref, cb_ref, cw_ref, frac_ref, u_ref, term_ref, a_ref=None, b_ref=None
):
    row_a = first_row(first)
    fraction = frac_ref[...]
    for message, start, e in ((from_a, SEG, first[1]), (from_b, SEG + 2 * CAP, 2 - first[1])):
        scale = cw_ref[pl.ds(start, CAP), :]
        for m in range(2):
            blocks = message[pl.ds(m * SEG + CAP, CAP), :]
            term_ref[pl.ds(m * CAP, CAP), :] = terms(blocks, fraction, scale)
        scatter(src, count, 1, e, u_ref, term_ref, 0, CAP)

    def add(s, message_a, message_b, at, to_a, to_b):
        own = pl.ds(s * COLS, COLS)
        for m in range(2):
            for row, scale, message, to in ((row_a, ca_ref, message_a, to_a), (ROW - 1 - row_a, cb_ref, message_b, to_b)):
                value = u_ref[row_at(m, s, row), :] + scale[own, :] * message[at(m), :]
                u_ref[row_at(m, s, row), :] = value
                if to is not None:
                    to[at(m), :] = value

    loop(INNER, lambda i: add(i + 1, rows_a, rows_b, lambda m: cols_at(m, i + 1), a_ref, b_ref))
    for q, s in enumerate((0, SEC - 1)):
        add(s, from_a, from_b, lambda m: edge_at(m, q), None, None)


def tile_kernel(
    src, count, first, u_in, from_a, from_b, rows_a, rows_b, ca_ref, cb_ref, cw_ref, frac_ref, u_ref, a_ref, b_ref, term_ref
):
    tile_adds(
        src, count, first, from_a, from_b, rows_a, rows_b, ca_ref, cb_ref, cw_ref, frac_ref, u_ref, term_ref, a_ref, b_ref
    )


def write_section(s, u_ref, held_ref, out_ref, sem):
    for m in range(2):
        for j in range(COLS):
            at = pl.ds(pl.multiple_of(PAD + m * PART + s * SECTION + j * ROW, 8), ROW)
            held_ref[m, s, :, lanes(j)] = u_ref[at, :]
        pltpu.make_async_copy(held_ref.at[m, s], out_ref.at[m, s], sem).start()


def last_tile_kernel(
    src, count, first, u_in, from_a, from_b, rows_a, rows_b, ca_ref, cb_ref, cw_ref, frac_ref, u_ref, out_ref, term_ref, held_ref, sem
):
    tile_adds(src, count, first, from_a, from_b, rows_a, rows_b, ca_ref, cb_ref, cw_ref, frac_ref, u_ref, term_ref)
    loop(INNER, lambda i: write_section(i + 1, u_ref, held_ref, out_ref, sem))
    inner = (slice(None), pl.ds(1, INNER))
    pltpu.make_async_copy(held_ref.at[inner], out_ref.at[inner], sem).wait()


def section_adds(src, count, first, from_a, from_b, cw_ref, frac_ref, u_ref, term_ref):
    fraction = frac_ref[...]
    for message, start, a in ((from_a, 0, first[0]), (from_b, 2 * SEG, 2 - first[0])):
        scale = cw_ref[pl.ds(start, SEG), :]
        for m in range(2):
            at = pl.ds(m * SEG, SEG)
            term_ref[at, :] = terms(message[at, :], fraction, scale)
        for j, e in enumerate((first[1], 1, 2 - first[1])):
            scatter(src, count, a, e, u_ref, term_ref, j * CAP, SEG)


def finish_kernel(src, count, wanted, first, u_in, from_a, from_b, cw_ref, frac_ref, u_ref, a_ref, b_ref, term_ref):
    section_adds(src, count, first, from_a, from_b, cw_ref, frac_ref, u_ref, term_ref)
    pack_messages(wanted, first, u_ref, a_ref, b_ref)


def last_kernel(src, count, first, u_in, out_in, from_a, from_b, cw_ref, frac_ref, u_ref, out_ref, term_ref, held_ref, sem):
    section_adds(src, count, first, from_a, from_b, cw_ref, frac_ref, u_ref, term_ref)
    for q, s in enumerate((0, SEC - 1)):
        for m in range(2):
            for j in range(COLS):
                held_ref[q, m, :, lanes(j)] = u_ref[pl.ds(PAD + m * PART + s * SECTION + j * ROW, ROW), :]
            pltpu.make_async_copy(held_ref.at[q, m], out_ref.at[m, s], sem.at[q, m]).start()
    for q, s in enumerate((0, SEC - 1)):
        for m in range(2):
            pltpu.make_async_copy(held_ref.at[q, m], out_ref.at[m, s], sem.at[q, m]).wait()


def on_device(
    displacement,
    stiff_right,
    stiff_down,
    bilinear,
    match_source,
    match_target,
    match_count,
    match_weight,
):
    tile_count = lax.axis_size("tile")
    sec, tile = lax.axis_index("sec"), lax.axis_index("tile")
    first = jnp.stack([2 - 2 * (sec % 2), 2 - 2 * (tile % 2), jnp.minimum(tile, 1)]).astype(jnp.int32)
    keep = jnp.where(tile == tile_count - 1, 0.0, 1.0).astype(jnp.float32).reshape(1)
    fraction = jnp.where(jnp.arange(LANE) == LANE - 1, 0.0, bilinear).reshape(1, LANE)

    displacement, stiff_right, stiff_down = (
        pltpu.with_memory_space_constraint(x, pltpu.HBM) for x in (displacement, stiff_right, stiff_down)
    )
    asked_a, asked_b = exchange(match_target, match_target, "sec")
    which = lax.broadcasted_iota(jnp.int32, (2,) + match_source.shape[1:], 0)
    ids = flat(jnp.where(which == 0, match_source, match_target))
    source = ids.reshape(-1)
    asked_a, asked_b = flat(asked_a), flat(asked_b)
    rows = [vmem(ROW_MSG, LANE), vmem(ROW_MSG, LANE)]
    field = vmem(FIELD, LANE)
    u, rim = kernel_call(
        load_kernel,
        [field, vmem(RIM, LANE)],
        [SM, ANY, HB, HB],
        scratch=[vmem(2, SEC, ROW, WID), vmem(SEC, WID), pltpu.SemaphoreType.DMA((3, 4))],
        cost=6_000_000,
        limit=8,
    )(keep, source, displacement, stiff_down)

    def pick(array, a, e):
        return lax.dynamic_slice(array, (0, a, e, 0), (1, 1, 1, CAP)).reshape(CAP)

    def request(e):
        asked = jnp.concatenate([pick(asked_a, 2 - first[0], e), pick(ids[1:], 1, e), pick(asked_b, first[0], e)])
        asked = jnp.pad(asked.astype(jnp.float32).reshape(1, SEG), ((0, 7), (0, LANE - SEG)))
        return jnp.concatenate([rim, asked], axis=0)

    got_a, got_b = exchange(request(first[1]), request(2 - first[1]), "tile")
    wanted = jnp.concatenate([got_a[RIM, :SEG], got_b[RIM, :SEG]]).astype(jnp.int32)
    wanted_sec = jnp.concatenate([pick(asked_a, 2 - first[0], 1), pick(asked_b, first[0], 1)])
    u, kr, kd, dg, rows_to_a, rows_to_b = kernel_call(
        setup_kernel,
        [field, vmem(PART, LANE), vmem(PART + 2 * PAD, LANE), vmem(PART, LANE), *rows],
        [SM, SM, SM, VM, HB, HB],
        aliases={3: 0},
        scratch=[vmem(SEC, ROW, WID), vmem(SEC, ROW, WID), pltpu.SemaphoreType.DMA((2, 4))],
        cost=6_000_000,
        limit=8,
    )(first, wanted_sec, keep, u, stiff_right, stiff_down)
    rows_a, rows_b = exchange(rows_to_a, rows_to_b, "tile")
    dg, u, cc = kernel_call(
        diagonal_kernel,
        [vmem(PART, LANE), field, vmem(PART, LANE)],
        [SM, SM, SM, VM, VM],
        aliases={3: 0, 4: 1},
        cost=4_000_000,
    )(source, match_weight, match_count, dg, u)
    messages = [vmem(T_MSG, LANE), vmem(T_MSG, LANE)]
    u, to_a, to_b = kernel_call(pack_kernel, [field, *messages], [SM, SM, VM], aliases={2: 0}, cost=1_000_000)(
        wanted, first, u
    )
    cc, u, ca, cb, cw = kernel_call(
        coefficient_kernel,
        [vmem(PART, LANE), field, vmem(RIM, LANE), vmem(RIM, LANE), vmem(9 * CAP, LANE)],
        [SM] * 4 + [VM] * 6,
        aliases={8: 0, 9: 1},
        cost=1_000_000,
    )(source, match_weight, match_count, first, dg, got_a, got_b, rim, cc, u)

    whole = jax.ShapeDtypeStruct(displacement.shape, jnp.float32)
    for step in range(ITERS):
        tile_a, tile_b = exchange(to_a, to_b, "tile")
        v, own_a, own_b = kernel_call(
            dense_kernel,
            [field, vmem(2 * CAP, LANE), vmem(2 * CAP, LANE)],
            [SM] * 3 + [VM] * 6,
            scratch=[vmem(2 * CAP, LANE)],
            cost=20_000_000,
        )(source, match_count, wanted_sec, u, kr, kd, cc, cw, fraction)
        sec_to_a, sec_to_b = kernel_call(relay_kernel, [vmem(2 * SEG, LANE)] * 2, [VM] * 4, cost=200_000)(
            tile_a, tile_b, own_a, own_b
        )
        sec_a, sec_b = exchange(sec_to_a, sec_to_b, "sec")
        received = (tile_a, tile_b, rows_a, rows_b, ca, cb, cw, fraction)
        if step + 1 < ITERS:
            v, *rows_to = kernel_call(
                tile_kernel,
                [field] + rows,
                [SM] * 3 + [VM] * 9,
                aliases={3: 0},
                scratch=[vmem(2 * CAP, LANE)],
                cost=2_000_000,
            )(source, match_count, first, v, *received)
            rows_a, rows_b = exchange(*rows_to, "tile")
            u, to_a, to_b = kernel_call(
                finish_kernel,
                [field] + messages,
                [SM] * 4 + [VM] * 5,
                aliases={4: 0},
                scratch=[vmem(2 * SEG, LANE)],
                cost=2_000_000,
            )(source, match_count, wanted, first, v, sec_a, sec_b, cw, fraction)
        else:
            v, out = kernel_call(
                last_tile_kernel,
                [field, whole],
                [SM] * 3 + [VM] * 9,
                aliases={3: 0},
                scratch=[vmem(2 * CAP, LANE), vmem(2, SEC, ROW, WID), pltpu.SemaphoreType.DMA],
                cost=4_000_000,
                out_specs=(VM, HB),
                limit=8,
            )(source, match_count, first, v, *received)
            _, out = kernel_call(
                last_kernel,
                [field, whole],
                [SM] * 3 + [VM, HB] + [VM] * 4,
                aliases={3: 0, 4: 1},
                scratch=[vmem(2 * SEG, LANE), vmem(2, 2, ROW, WID), pltpu.SemaphoreType.DMA((2, 2))],
                cost=2_000_000,
                out_specs=(VM, HB),
            )(source, match_count, first, v, out, sec_a, sec_b, cw, fraction)
    return out


def solution(mesh):
    in_specs = (
        P(None, "sec", "tile", None),
        P("sec", "tile", None),
        P("sec", "tile", None),
        P(),
        P(("sec", "tile"), None, None, None),
        P(("sec", "tile"), None, None, None),
        P(("sec", "tile"), None, None),
        P(("sec", "tile"), None, None, None),
    )
    out_specs = P(None, "sec", "tile", None)
    return jax.shard_map(
        on_device, mesh=mesh, in_specs=in_specs, out_specs=out_specs, check_vma=False
    )
```
